512 devices in a mesh: tensor: 8 (over x, core), wide: 64 (over z, y).
Axes of the slice: x: 4, y: 4, z: 16, core: 2. Of those that a mesh axis runs over, the one named last changes fastest.
Arguments:
- tokens: bfloat16 [512, 3072], P('wide', 'tensor'), may hold values from -6 to 6
- cotangent: bfloat16 [512, 3072], P('wide', 'tensor'), may hold values from -1.5 to 1.5
- gates: bfloat16 [512, 2], P('wide'), may hold values from 0.19921875 to 1
- experts: int32 [512, 2], P('wide'), may hold values from 0 to 7, all different within a row; in each aligned block of 8 rows (0 to 7, 8 to 15, ...) at most 4 rows name the same one
- w_gate: bfloat16 [64, 3072, 1024], P('wide', None, 'tensor'), may hold values from -0.109375 to 0.109375
- w_up: bfloat16 [64, 3072, 1024], P('wide', None, 'tensor'), may hold values from -0.109375 to 0.109375
- w_down: bfloat16 [64, 1024, 3072], P('wide', 'tensor'), may hold values from -0.0625 to 0.0625
Outputs:
- input_grad: bfloat16 [512, 3072], P('wide', 'tensor')
- routing_grad: float32 [512, 2], P('wide')
- gate_proj_grad: bfloat16 [64, 3072, 1024], P('wide', None, 'tensor')
- up_proj_grad: bfloat16 [64, 3072, 1024], P('wide', None, 'tensor')
- down_proj_grad: bfloat16 [64, 1024, 3072], P('wide', 'tensor')
The draws below stay inside these ranges and needn't reach their ends.
Inputs may be any that keep to these rules, and one draw needn't show every extreme that they name: Each token names 2 different experts. Among the 8 tokens of one index of wide (aligned blocks of rows) no expert is named more than 4 times, and in every draw some expert is named exactly 4 times by some block.
All inputs are finite; a program needn't handle non-finite values.
Results may differ from the reference program's by a relative error of at most 0.02.
Values may be sent and summed in bfloat16 or wider, within the bound.
A program may use at most 64 MiB of HBM per device.

```python
import math
import jax
import jax.numpy as jnp
import numpy as np

D = 3072
FF = 8192
E = 8
TOP = 2
TOK_DEV = 8
CAP = 4
FFR = 1024
SLABS = 64
TOKENS = 512
N_WIDE = 64


def levels(own_key, shape, pieces, low, high):
    loudness, own = 1.0, jax.random.fold_in(own_key, 6)
    for dim, shards_of in pieces:
        heights = jnp.exp(jax.random.uniform(jax.random.fold_in(own, dim), (shards_of,), jnp.float32, low / len(pieces), high / len(pieces)))
        loudness = loudness * jnp.repeat(heights, shape[dim] // shards_of).reshape([-1 if axis == dim else 1 for axis in range(len(shape))])
    return loudness


def shared_out(stream_key, own, number, rows, count, top, limit, skew):
    ranking = jax.random.permutation(stream_key, count)
    crowded, usual = shares(count, rows * top, limit, skew, True), shares(count, rows * top, limit, skew, False)
    places = jnp.arange(count)

    def named(sizes, offset_by):
        used = int((sizes > 0).sum())
        fixed = max(1, used // 4)
        passed = fixed + (places - fixed + offset_by * (used - fixed)) % max(1, count - fixed)
        return jnp.zeros((count,), jnp.int32).at[ranking[jnp.where(places < fixed, places, passed)]].set(jnp.asarray(sizes, jnp.int32))

    sizes = jnp.where(number % 4 == 0, named(crowded, number // 4), named(usual, number - number // 4 - 1))
    mixed = jax.random.permutation(jax.random.fold_in(own, 3), count)
    donor, taker = mixed[0:count // 2 * 2:2], mixed[1:count // 2 * 2:2]
    room = jnp.minimum(sizes[donor] - 1, limit - sizes[taker]) // 2
    room = jnp.where((donor == ranking[0]) | (taker == ranking[0]) | (sizes[taker] == 0), 0, jnp.maximum(room, 0))
    passed = jax.random.randint(jax.random.fold_in(own, 4), (count // 2,), 0, 1 << 20) % (room + 1)
    sizes = sizes.at[donor].add(-passed).at[taker].add(passed)
    labels = jnp.searchsorted(jnp.cumsum(sizes), jnp.arange(rows * top), side="right").astype(jnp.int32)
    grid = labels.reshape(top, rows).T
    grid = grid[jax.random.permutation(jax.random.fold_in(own, 1), rows)]
    offset_by = jax.random.randint(jax.random.fold_in(own, 2), (rows, 1), 0, top)
    return jnp.take_along_axis(grid, (jnp.arange(top)[None, :] + offset_by) % top, axis=1)


def shares(amount, total, most, lean, full):
    weights = [(1 << 20) // math.isqrt(standing ** lean) + 1 for standing in range(1, amount + 1)]
    largest = most if full else min(most, max(-(-total // amount), total * weights[0] // sum(weights)))
    least = 1 if total - largest >= amount - 1 else 0
    given, rest = [largest] + [least] * (amount - 1), total - largest - least * (amount - 1)
    while rest > 0:
        free = [i for i in range(1, amount) if given[i] < largest] or [i for i in range(1, amount) if given[i] < most]
        whole, budget = sum([weights[i] for i in free]), rest
        for i in free:
            extra = min(most - given[i], max(1, budget * weights[i] // whole), rest)
            given[i] = given[i] + extra
            rest = rest - extra
    return np.array(given)


def gaussian(stream_key, shape, spread, limit, shards=(), kind=jnp.bfloat16):
    gain = levels(stream_key, shape, shards, -0.22, 0.18) if shards else 1.0
    drawn = jax.random.normal(stream_key, shape, jnp.float32) * spread * gain
    return jnp.minimum(jnp.maximum(drawn, -limit), limit).astype(kind)


def setup_inputs(seed: int = 0) -> dict:
    streams_of = jax.random.split(jax.random.key(seed), 8)
    tokens = gaussian(streams_of[0], (TOKENS, D), 1.0, 6.0, ((0, 64), (1, 8)))
    cotangent = gaussian(streams_of[1], (TOKENS, D), 0.25, 1.5, ((0, 64), (1, 8)))
    gates = jnp.clip(0.19921875 + 0.80078125 * jax.random.uniform(streams_of[2], (TOKENS, TOP), jnp.float32) ** levels(streams_of[2], (TOKENS, TOP), ((0, 64),), -0.2, 0.2), 0.19921875, 1.0).astype(jnp.bfloat16)
    experts_keys = jax.random.split(jax.random.fold_in(streams_of[3], 1), TOKENS // TOK_DEV)
    experts_turns = jax.random.permutation(jax.random.fold_in(streams_of[3], 3), TOKENS // TOK_DEV)
    experts = jax.vmap(lambda own, number: shared_out(jax.random.fold_in(streams_of[3], 2), own, number, TOK_DEV, E, TOP, CAP, 2))(experts_keys, experts_turns).reshape((TOKENS, TOP))
    w_gate = gaussian(streams_of[4], (SLABS, D, FFR), D ** -0.5, 0.109375, ((0, 64), (2, 8)))
    w_up = gaussian(streams_of[5], (SLABS, D, FFR), D ** -0.5, 0.109375, ((0, 64), (2, 8)))
    w_down = gaussian(streams_of[6], (SLABS, FFR, D), FF ** -0.5, 0.0625, ((0, 64), (1, 8)))
    return {"tokens": tokens, "cotangent": cotangent, "gates": gates, "experts": experts, "w_gate": w_gate, "w_up": w_up, "w_down": w_down}


def reference(tokens, cotangent, gates, experts, w_gate, w_up, w_down):
    slot_rows = N_WIDE * CAP
    replicas = N_WIDE // E
    hidden_all = FFR * replicas
    gate_full = w_gate.reshape(E, replicas, D, FFR).transpose(0, 2, 1, 3).reshape(E, D, hidden_all)
    up_full = w_up.reshape(E, replicas, D, FFR).transpose(0, 2, 1, 3).reshape(E, D, hidden_all)
    down_full = w_down.reshape(E, hidden_all, D)
    input_grad = jnp.zeros((TOKENS, D), jnp.float32)
    routing_grad = jnp.zeros((TOKENS, TOP), jnp.float32)
    gate_grads = []
    up_grads = []
    down_grads = []
    for expert in range(E):
        chosen = experts == expert
        picked = jnp.any(chosen, axis=1)
        weight = jnp.sum(jnp.where(chosen, gates.astype(jnp.float32), 0.0), axis=1)
        where_rows = jnp.nonzero(picked, size=slot_rows, fill_value=0)[0]
        live_rows = (jnp.arange(slot_rows) < jnp.sum(picked.astype(jnp.int32))).astype(jnp.float32)
        inputs = tokens[where_rows]
        upstream = cotangent[where_rows]
        slot_scale = weight[where_rows] * live_rows
        pre_gate = jnp.dot(inputs, gate_full[expert], preferred_element_type=jnp.float32)
        pre_up = jnp.dot(inputs, up_full[expert], preferred_element_type=jnp.float32)
        sigmoid_gate = jax.nn.sigmoid(pre_gate)
        active = pre_gate * sigmoid_gate
        hidden = active * pre_up
        weighted = (slot_scale[:, None] * hidden).astype(jnp.bfloat16)
        through = jnp.dot(upstream, down_full[expert].T, preferred_element_type=jnp.float32)
        gate_terms = jnp.sum(through * hidden, axis=1) * live_rows
        hidden_grad = slot_scale[:, None] * through
        grad_pre_gate = (hidden_grad * pre_up * sigmoid_gate * (1.0 + pre_gate * (1.0 - sigmoid_gate))).astype(jnp.bfloat16)
        grad_pre_up = (hidden_grad * active).astype(jnp.bfloat16)
        gate_grads.append(jnp.dot(inputs.T, grad_pre_gate, preferred_element_type=jnp.float32).astype(jnp.bfloat16))
        up_grads.append(jnp.dot(inputs.T, grad_pre_up, preferred_element_type=jnp.float32).astype(jnp.bfloat16))
        down_grads.append(jnp.dot(weighted.T, upstream, preferred_element_type=jnp.float32).astype(jnp.bfloat16))
        returned = jnp.dot(grad_pre_gate, gate_full[expert].T, preferred_element_type=jnp.float32)
        returned = returned + jnp.dot(grad_pre_up, up_full[expert].T, preferred_element_type=jnp.float32)
        input_grad = input_grad.at[where_rows].add(returned * live_rows[:, None])
        routing_grad = routing_grad.at[where_rows].add(jnp.where(chosen[where_rows], gate_terms[:, None], 0.0))
    gate_stack = jnp.stack(gate_grads).reshape(E, D, replicas, FFR).transpose(0, 2, 1, 3).reshape(E * replicas, D, FFR)
    up_stack = jnp.stack(up_grads).reshape(E, D, replicas, FFR).transpose(0, 2, 1, 3).reshape(E * replicas, D, FFR)
    down_stack = jnp.stack(down_grads).reshape(E * replicas, FFR, D)
    return (input_grad.astype(jnp.bfloat16), routing_grad, gate_stack, up_stack, down_stack)
```

```python
import jax
import jax.numpy as jnp
from jax import lax
from jax.experimental import pallas as pl
from jax.experimental.pallas import tpu as pltpu
from jax.sharding import PartitionSpec as P

MESH = pl.DeviceIdType.MESH
NZ, NY, NX = 16, 4, 4
TOK = 8
D = 3072
FEAT = 384
HID = 128
ROWS = 64
SLOTS = 256
BF = jnp.bfloat16
F32 = jnp.float32
VMEM = pl.BlockSpec(memory_space=pltpu.VMEM)


def position():
    tensor, wide = lax.axis_index("tensor"), lax.axis_index("wide")
    return (
        lax.div(tensor, 2),
        lax.rem(tensor, 2),
        lax.div(wide, NY),
        lax.rem(wide, NY),
    )


def device_of(x, core, z, y):
    return {"tensor": x * 2 + core, "wide": z * NY + y}


def wrap(value, size):
    return lax.rem(value + size, size)


def dot(left, right, left_dim, right_dim):
    return lax.dot_general(
        left, right, (((left_dim,), (right_dim,)), ((), ())), preferred_element_type=F32
    )


def meet(partners):
    barrier = pltpu.get_barrier_semaphore()
    for partner in partners:
        pl.semaphore_signal(barrier, inc=1, device_id=partner, device_id_type=MESH)
    pl.semaphore_wait(barrier, len(partners))


class Wire:
    def __init__(self, send_sem, recv_sem):
        self.send_sem, self.recv_sem = send_sem, recv_sem
        self.sent = []

    def make(self, number, source, target, device):
        return pltpu.make_async_remote_copy(
            src_ref=source,
            dst_ref=target,
            send_sem=self.send_sem.at[number],
            recv_sem=self.recv_sem.at[number],
            device_id=device,
            device_id_type=MESH,
        )

    def send(self, number, source, target, device):
        copy = self.make(number, source, target, device)
        copy.start()
        self.sent.append(copy)

    def arrived(self, number, landed, device):
        self.make(number, landed, landed, device).wait_recv()

    def drain(self):
        for copy in self.sent:
            copy.wait_send()


def slot_match(experts, lanes, per_expert):
    lane = lax.broadcasted_iota(jnp.int32, (TOK, lanes), 1)
    expert, half, slot = lane // per_expert, (lane // 4) % 2, lane % 4
    first = jnp.broadcast_to(experts[:, 0:1], (TOK, lanes)) == expert
    second = jnp.broadcast_to(experts[:, 1:2], (TOK, lanes)) == expert
    one, zero = jnp.ones((TOK, lanes), F32), jnp.zeros((TOK, lanes), F32)
    first, second = jnp.where(first, one, zero), jnp.where(second, one, zero)
    row = lax.broadcasted_iota(jnp.int32, (TOK, TOK), 0)
    column = lax.broadcasted_iota(jnp.int32, (TOK, TOK), 1)
    earlier = jnp.where(column < row, 1.0, 0.0).astype(F32)
    before = dot(earlier, first + second, 1, 0)
    at_slot = jnp.where(before == slot.astype(F32), one, zero)
    upper = jnp.where(half == 0, one, zero)
    return first * at_slot, second * at_slot, upper


def dispatch_kernel(
    tokens_ref,
    cotangent_ref,
    gates_ref,
    experts_ref,
    x_ref,
    c_ref,
    g_ref,
    out_buf,
    in_buf,
    z_send,
    z_recv,
    send_sem,
    recv_sem,
):
    x, core, z, y = position()
    peers_z = [device_of(x, core, wrap(z + d, NZ), y) for d in range(1, NZ)]
    x_next, x_prev = device_of(wrap(x + 1, NX), core, z, y), device_of(wrap(x - 1, NX), core, z, y)
    y_next, y_prev = device_of(x, core, z, wrap(y + 1, NY)), device_of(x, core, z, wrap(y - 1, NY))
    y_far = device_of(x, core, z, wrap(y + 2, NY))
    sibling = device_of(x, 1 - core, z, y)
    meet(peers_z + [x_next, x_prev, y_next, y_prev, y_far, sibling])

    first, second, upper = slot_match(experts_ref[...], 64, 8)
    gates = gates_ref[...].astype(F32)
    either = first + second
    pick_in = (either * upper).astype(BF)
    pick_up = (either * (1.0 - upper)).astype(BF)
    chosen = dot(pick_in, tokens_ref[...], 0, 0) + dot(pick_up, cotangent_ref[...], 0, 0)
    gate_at = first * gates[:, 0:1] + second * gates[:, 1:2]
    gate_rows = dot(gate_at.astype(BF), jnp.ones((TOK, 128), BF), 0, 0)
    out_buf[:, :, 0:FEAT] = chosen.reshape(8, 8, FEAT).astype(BF)
    out_buf[:, :, FEAT:] = gate_rows.reshape(8, 8, 128).astype(BF)

    zwire = Wire(z_send, z_recv)
    for d in (8, 7, 9, 6, 10, 5, 11, 4, 12, 3, 13, 2, 14, 1, 15):
        there = wrap(z + d, NZ)
        zwire.send(
            d - 1, out_buf.at[lax.div(there, 2)], in_buf.at[z], device_of(x, core, there, y)
        )
    in_buf[z] = out_buf[lax.div(z, 2)]
    for d in range(1, NZ):
        zwire.arrived(d - 1, in_buf.at[wrap(z - d, NZ)], sibling)

    out_row = lax.broadcasted_iota(jnp.int32, (128, 128), 0)
    in_row = lax.broadcasted_iota(jnp.int32, (128, 128), 1)
    wanted = (out_row % 64) // 4 * 8 + out_row // 64 * 4 + out_row % 4
    order = jnp.where(in_row == wanted, 1.0, 0.0).astype(BF)
    came = in_buf[...].astype(F32).reshape(128, FEAT + 128).astype(BF)
    sorted_rows = dot(order, came, 1, 0).astype(BF)

    def block(ref, xi, ci, yi, start=0, count=ROWS):
        return ref.at[
            pl.ds(pl.multiple_of(yi * ROWS + start, 32), count),
            pl.ds(pl.multiple_of((xi * 2 + ci) * FEAT, 128), FEAT),
        ]

    my_rows = pl.ds(pl.multiple_of(y * ROWS, ROWS), ROWS)
    my_columns = pl.ds(pl.multiple_of((x * 2 + core) * FEAT, 128), FEAT)
    x_ref[my_rows, my_columns] = sorted_rows[0:64, 0:FEAT]
    c_ref[my_rows, my_columns] = sorted_rows[64:128, 0:FEAT]
    g_ref[my_rows, :] = sorted_rows[0:64, FEAT:]

    wire = Wire(send_sem, recv_sem)

    class Gather:
        def __init__(self, ref, base, first_axis):
            self.ref, self.base = ref, base
            if first_axis == "x":
                self.a, self.b = x, y
                self.up, self.down, self.fore, self.back = x_next, x_prev, y_next, y_prev
            else:
                self.a, self.b = y, x
                self.up, self.down, self.fore, self.back = y_next, y_prev, x_next, x_prev
            self.swap = first_axis != "x"

        def at(self, a, b, ci, start=0, count=ROWS):
            a, b = wrap(self.a + a, 4), wrap(self.b + b, 4)
            xi, yi = (b, a) if self.swap else (a, b)
            return block(self.ref, xi, ci, yi, start, count)

        def push(self, number, piece, device):
            wire.send(self.base + number, piece, piece, device)

        def got(self, number, piece):
            wire.arrived(self.base + number, piece, sibling)

        def start(self):
            own = self.at(0, 0, core)
            self.push(0, own, self.up)
            self.push(1, own, self.down)

        def spread(self, k, a):
            own = self.at(a, 0, core)
            self.push(4 + 4 * k, own, self.fore)
            self.push(5 + 4 * k, own, self.back)
            self.push(20 + 4 * k, own, sibling)

        def first_near(self):
            self.got(0, self.at(-1, 0, core))
            self.push(2, self.at(-1, 0, core, 0, 32), self.up)
            self.spread(1, -1)
            self.got(1, self.at(1, 0, core))
            self.push(3, self.at(1, 0, core, 32, 32), self.down)
            self.spread(2, 1)

        def first_far(self):
            self.got(2, self.at(2, 0, core, 0, 32))
            self.got(3, self.at(2, 0, core, 32, 32))
            self.spread(3, 2)

        def second_near(self, k, a):
            self.got(4 + 4 * k, self.at(a, -1, core))
            self.push(6 + 4 * k, self.at(a, -1, core, 0, 32), self.fore)
            self.push(21 + 4 * k, self.at(a, -1, core), sibling)
            self.got(5 + 4 * k, self.at(a, 1, core))
            self.push(7 + 4 * k, self.at(a, 1, core, 32, 32), self.back)
            self.push(22 + 4 * k, self.at(a, 1, core), sibling)

        def second_far(self, k, a):
            self.got(6 + 4 * k, self.at(a, 2, core, 0, 32))
            self.got(7 + 4 * k, self.at(a, 2, core, 32, 32))
            self.push(23 + 4 * k, self.at(a, 2, core), sibling)

        def from_sibling(self):
            for k, a in enumerate((0, -1, 1, 2)):
                for m, b in enumerate((0, -1, 1, 2)):
                    self.got(20 + 4 * k + m, self.at(a, b, 1 - core))

    gathers = (Gather(x_ref, 0, "x"), Gather(c_ref, 36, "y"))
    for one in gathers:
        one.start()
    for one in gathers:
        one.spread(0, 0)
    gate_block = g_ref.at[my_rows, :]
    for number, device in enumerate((y_next, y_prev, y_far)):
        wire.send(72 + number, gate_block, gate_block, device)
    for one in gathers:
        one.first_near()
    for one in gathers:
        one.second_near(0, 0)
    for one in gathers:
        one.first_far()
    for k, a in ((1, -1), (2, 1)):
        for one in gathers:
            one.second_near(k, a)
        for one in gathers:
            one.second_far(k - 1, (0, -1)[k - 1])
    for one in gathers:
        one.second_near(3, 2)
    for one in gathers:
        one.second_far(2, 1)
    for one in gathers:
        one.second_far(3, 2)
    for one in gathers:
        one.from_sibling()
    for number, d in enumerate((-1, 1, 2)):
        landed = g_ref.at[pl.ds(pl.multiple_of(wrap(y + d, NY) * ROWS, ROWS), ROWS), :]
        wire.arrived(72 + number, landed, sibling)
    zwire.drain()
    wire.drain()


def dispatch(tokens, cotangent, gates, experts):
    return pl.pallas_call(
        dispatch_kernel,
        name="dispatch",
        out_shape=(
            jax.ShapeDtypeStruct((SLOTS, D), BF),
            jax.ShapeDtypeStruct((SLOTS, D), BF),
            jax.ShapeDtypeStruct((SLOTS, 128), BF),
        ),
        in_specs=[VMEM] * 4,
        out_specs=(VMEM,) * 3,
        scratch_shapes=[
            pltpu.VMEM((8, 8, FEAT + 128), BF),
            pltpu.VMEM((NZ, 8, FEAT + 128), BF),
            pltpu.SemaphoreType.DMA((NZ - 1,)),
            pltpu.SemaphoreType.DMA((NZ - 1,)),
            pltpu.SemaphoreType.DMA((75,)),
            pltpu.SemaphoreType.DMA((75,)),
        ],
        compiler_params=pltpu.CompilerParams(
            collective_id=0, has_side_effects=True, vmem_limit_bytes=24 << 20
        ),
    )(tokens, cotangent, gates, experts)


def layer_kernel(
    x_ref, c_ref, g_ref, wg_ref, wu_ref, wd_ref, dwg_ref, dwu_ref, dwd_ref, r_ref, t_ref
):
    scale = g_ref[...].astype(F32)
    pre_gate = dot(x_ref[...], wg_ref[0], 1, 0)
    pre_up = dot(x_ref[...], wu_ref[0], 1, 0)
    through = dot(c_ref[...], wd_ref[0], 1, 1)
    sig = jax.nn.sigmoid(pre_gate)
    act = pre_gate * sig
    hidden = act * pre_up
    weighted = (scale * hidden).astype(BF)
    hidden_grad = scale * through
    grad_gate = (hidden_grad * pre_up * sig * (1.0 + pre_gate * (1.0 - sig))).astype(BF)
    grad_up = (hidden_grad * act).astype(BF)

    row = lax.broadcasted_iota(jnp.int32, (ROWS, 128), 0)
    lane = lax.broadcasted_iota(jnp.int32, (ROWS, 128), 1)
    sums = jnp.sum(through * hidden, axis=1, keepdims=True)
    for yi in range(NY):
        part = jnp.broadcast_to(sums[yi * ROWS : (yi + 1) * ROWS], (ROWS, 128))
        line = jnp.sum(jnp.where(row == lane, part, 0.0), axis=0, keepdims=True)
        t_ref[yi] = jnp.broadcast_to(line, (8, 128))

    step = 512
    for k in range(D // step):
        rows = pl.ds(k * step, step)
        r_ref[:, rows] = (
            dot(grad_gate, wg_ref[0, rows, :], 1, 1) + dot(grad_up, wu_ref[0, rows, :], 1, 1)
        ).astype(BF)
        dwg_ref[0, rows, :] = dot(x_ref[:, rows], grad_gate, 0, 0).astype(BF)
        dwu_ref[0, rows, :] = dot(x_ref[:, rows], grad_up, 0, 0).astype(BF)
        dwd_ref[0, :, rows] = dot(weighted, c_ref[:, rows], 0, 0).astype(BF)


def layer(inputs, upstream, scale, w_gate, w_up, w_down):
    return pl.pallas_call(
        layer_kernel,
        name="layer",
        out_shape=(
            jax.ShapeDtypeStruct((1, D, HID), BF),
            jax.ShapeDtypeStruct((1, D, HID), BF),
            jax.ShapeDtypeStruct((1, HID, D), BF),
            jax.ShapeDtypeStruct((SLOTS, D), BF),
            jax.ShapeDtypeStruct((NY, 8, 128), F32),
        ),
        in_specs=[VMEM] * 6,
        out_specs=(VMEM,) * 5,
        compiler_params=pltpu.CompilerParams(vmem_limit_bytes=40 << 20),
    )(inputs, upstream, scale, w_gate, w_up, w_down)


def combine_kernel(
    r_ref,
    t_ref,
    experts_ref,
    grad_ref,
    routing_ref,
    sib_buf,
    acc_p,
    acc_q,
    near_p,
    near_q,
    full_p,
    full_q,
    mid_p,
    mid_q,
    last_p,
    last_q,
    t_y,
    t_sum,
    t_t,
    out_buf,
    in_buf,
    z_send,
    z_recv,
    send_sem,
    recv_sem,
):
    x, core, z, y = position()
    tensor = x * 2 + core
    peers_z = [device_of(x, core, wrap(z + d, NZ), y) for d in range(1, NZ)]
    peers_t = [{"tensor": wrap(tensor + d, 8), "wide": z * NY + y} for d in range(1, 8)]
    peers_y = [device_of(x, core, z, wrap(y + d, NY)) for d in range(1, NY)]
    peers_x = [device_of(wrap(x + d, NX), core, z, y) for d in range(1, NX)]
    sibling = device_of(x, 1 - core, z, y)
    meet(peers_z + peers_t + peers_y)

    wire = Wire(send_sem, recv_sem)
    x_order = (2, 1, 3, 0)
    for k, d in enumerate(x_order):
        xi = wrap(x + d, NX)
        columns = pl.ds(pl.multiple_of((xi * 2 + 1 - core) * FEAT, 128), FEAT)
        wire.send(k, r_ref.at[:, columns], sib_buf.at[k], sibling)
    for d in range(1, NY):
        wire.send(3 + d, t_ref.at[wrap(y + d, NY)], t_y.at[d - 1], peers_y[d - 1])

    for k, d in enumerate(x_order):
        xi = wrap(x + d, NX)
        columns = pl.ds(pl.multiple_of((xi * 2 + core) * FEAT, 128), FEAT)
        wire.arrived(k, sib_buf.at[k], sibling)
        for yi in range(NY):
            rows = pl.ds(yi * ROWS, ROWS)
            total = (
                r_ref[rows, columns].astype(F32) + sib_buf[k, rows, :].astype(F32)
            ).astype(BF)
            acc_p[xi, yi] = total[0:32]
            acc_q[yi, xi] = total[32:64]

    class Scatter:
        def __init__(self, base, acc, near, full, mid, last, a, b, first_peers, second_peers):
            self.base, self.acc, self.near, self.full = base, acc, near, full
            self.mid, self.last, self.a, self.b = mid, last, a, b
            self.first_peers, self.second_peers = first_peers, second_peers

        def far(self):
            far = wrap(self.a + 2, 4)
            wire.send(
                self.base, self.acc.at[far, pl.ds(0, 2)], self.near.at[0], self.first_peers[0]
            )
            wire.send(
                self.base + 1, self.acc.at[far, pl.ds(2, 2)], self.near.at[1], self.first_peers[2]
            )

        def close(self):
            for side, chunk, peer in ((0, 1, 0), (1, 3, 2)):
                wire.arrived(self.base + side, self.near.at[side], sibling)
                there = wrap(self.a + chunk, 4)
                for i in range(2):
                    self.acc[there, 2 * side + i] = (
                        self.acc[there, 2 * side + i].astype(F32)
                        + self.near[side, i].astype(F32)
                    ).astype(BF)
                wire.send(
                    self.base + 2 + side,
                    self.acc.at[there],
                    self.full.at[side],
                    self.first_peers[peer],
                )

        def across(self):
            for side in range(2):
                wire.arrived(self.base + 2 + side, self.full.at[side], sibling)
            for i in range(4):
                self.mid[i] = (
                    self.acc[self.a, i].astype(F32)
                    + self.full[0, i].astype(F32)
                    + self.full[1, i].astype(F32)
                ).astype(BF)
            for d in range(1, 4):
                wire.send(
                    self.base + 3 + d,
                    self.mid.at[wrap(self.b + d, 4)],
                    self.last.at[d - 1],
                    self.second_peers[d - 1],
                )

        def total(self):
            result = self.mid[self.b].astype(F32)
            for d in range(1, 4):
                wire.arrived(self.base + 3 + d, self.last.at[d - 1], sibling)
                result = result + self.last[d - 1].astype(F32)
            return result

    scatters = (
        Scatter(7, acc_p, near_p, full_p, mid_p, last_p, x, y, peers_x, peers_y),
        Scatter(14, acc_q, near_q, full_q, mid_q, last_q, y, x, peers_y, peers_x),
    )
    for one in scatters:
        one.far()
    line = t_ref[y]
    for d in range(1, NY):
        wire.arrived(3 + d, t_y.at[d - 1], sibling)
        line = line + t_y[d - 1]
    t_sum[...] = line
    t_t[tensor] = line
    for d in range(1, 8):
        wire.send(20 + d, t_sum, t_t.at[tensor], peers_t[d - 1])
    for one in scatters:
        one.close()
    for one in scatters:
        one.across()
    for d in range(1, 8):
        wire.arrived(20 + d, t_t.at[wrap(tensor - d, 8)], sibling)
    line = t_t[0]
    for i in range(1, 8):
        line = line + t_t[i]
    row = lax.broadcasted_iota(jnp.int32, (ROWS, 128), 0)
    lane = lax.broadcasted_iota(jnp.int32, (ROWS, 128), 1)
    spread = jnp.where(row == lane, jnp.broadcast_to(line[0:1], (ROWS, 128)), 0.0)
    column = jnp.broadcast_to(jnp.sum(spread, axis=1, keepdims=True), (ROWS, 128))

    result = jnp.concatenate([one.total() for one in scatters], axis=0)
    pair = jnp.concatenate(
        [
            result[:, 0:256],
            jnp.concatenate([result[:, 256:FEAT], column], axis=1),
        ],
        axis=0,
    ).astype(BF)
    out_row = lax.broadcasted_iota(jnp.int32, (128, 128), 0)
    in_row = lax.broadcasted_iota(jnp.int32, (128, 128), 1)
    wanted = (out_row // 4) % 2 * 64 + out_row // 8 * 4 + out_row % 4
    order = jnp.where(in_row == wanted, 1.0, 0.0).astype(BF)
    out_buf[...] = dot(order, pair, 1, 0).reshape(NZ, 8, 256).astype(BF)

    zwire = Wire(z_send, z_recv)
    for d in (8, 7, 9, 6, 10, 5, 11, 4, 12, 3, 13, 2, 14, 1, 15):
        zwire.send(d - 1, out_buf.at[wrap(z + d, NZ)], in_buf.at[z], peers_z[d - 1])
    in_buf[z] = out_buf[z]
    first, second, upper = slot_match(experts_ref[...], 128, 16)
    for d in range(1, NZ):
        zwire.arrived(d - 1, in_buf.at[wrap(z - d, NZ)], sibling)
    came = in_buf[...].astype(F32).reshape(128, 256).astype(BF)
    either = first + second
    lower = 1.0 - upper
    head = dot((either * upper).astype(BF), came, 1, 0)
    tail = dot((either * lower).astype(BF), came[:, 0:128], 1, 0)
    grad_ref[:, 0:256] = head.astype(BF)
    grad_ref[:, 256:FEAT] = tail.astype(BF)
    at_first = dot((first * lower).astype(BF), came[:, 128:], 1, 0)
    at_second = dot((second * lower).astype(BF), came[:, 128:], 1, 0)
    which = lax.broadcasted_iota(jnp.int32, (TOK, 128), 1)
    routing_ref[...] = jnp.where(which == 0, at_first, at_second)[:, 0:2]
    zwire.drain()
    wire.drain()


def combine(returned, lines, experts):
    return pl.pallas_call(
        combine_kernel,
        name="combine",
        out_shape=(
            jax.ShapeDtypeStruct((TOK, FEAT), BF),
            jax.ShapeDtypeStruct((TOK, 2), F32),
        ),
        in_specs=[VMEM] * 3,
        out_specs=(VMEM,) * 2,
        scratch_shapes=[
            pltpu.VMEM((NX, SLOTS, FEAT), BF),
            pltpu.VMEM((4, 4, 32, FEAT), BF),
            pltpu.VMEM((4, 4, 32, FEAT), BF),
            pltpu.VMEM((2, 2, 32, FEAT), BF),
            pltpu.VMEM((2, 2, 32, FEAT), BF),
            pltpu.VMEM((2, 4, 32, FEAT), BF),
            pltpu.VMEM((2, 4, 32, FEAT), BF),
            pltpu.VMEM((4, 32, FEAT), BF),
            pltpu.VMEM((4, 32, FEAT), BF),
            pltpu.VMEM((3, 32, FEAT), BF),
            pltpu.VMEM((3, 32, FEAT), BF),
            pltpu.VMEM((3, 8, 128), F32),
            pltpu.VMEM((8, 128), F32),
            pltpu.VMEM((8, 8, 128), F32),
            pltpu.VMEM((NZ, 8, 256), BF),
            pltpu.VMEM((NZ, 8, 256), BF),
            pltpu.SemaphoreType.DMA((NZ - 1,)),
            pltpu.SemaphoreType.DMA((NZ - 1,)),
            pltpu.SemaphoreType.DMA((28,)),
            pltpu.SemaphoreType.DMA((28,)),
        ],
        compiler_params=pltpu.CompilerParams(
            collective_id=1, has_side_effects=True, vmem_limit_bytes=24 << 20
        ),
    )(returned, lines, experts)


def shards(tokens, cotangent, gates, experts, w_gate, w_up, w_down):
    inputs, upstream, scale = dispatch(tokens, cotangent, gates, experts)
    gate_grad, up_grad, down_grad, returned, lines = layer(
        inputs, upstream, scale, w_gate, w_up, w_down
    )
    input_grad, routing_grad = combine(returned, lines, experts)
    return input_grad, routing_grad, gate_grad, up_grad, down_grad


def solution(mesh):
    return jax.shard_map(
        shards,
        mesh=mesh,
        in_specs=(
            P("wide", "tensor"),
            P("wide", "tensor"),
            P("wide", None),
            P("wide", None),
            P("wide", None, "tensor"),
            P("wide", None, "tensor"),
            P("wide", "tensor", None),
        ),
        out_specs=(
            P("wide", "tensor"),
            P("wide", None),
            P("wide", None, "tensor"),
            P("wide", None, "tensor"),
            P("wide", "tensor", None),
        ),
        check_vma=False,
    )
```

```python
import jax
import jax.numpy as jnp
from jax import lax
from jax.experimental import pallas as pl
from jax.experimental.pallas import tpu as pltpu
from jax.sharding import PartitionSpec as P

MESH = pl.DeviceIdType.MESH
NZ, NY, NX = 16, 4, 4
TOK = 8
D = 3072
FEAT = 384
HID = 128
ROWS = 64
SLOTS = 256
BF = jnp.bfloat16
F32 = jnp.float32
VMEM = pl.BlockSpec(memory_space=pltpu.VMEM)
HBM = pl.BlockSpec(memory_space=pltpu.MemorySpace.HBM)
Z_ORDER = (8, 7, 9, 6, 10, 5, 11, 4, 12, 3, 13, 2, 14, 1, 15)


def position():
    tensor, wide = lax.axis_index("tensor"), lax.axis_index("wide")
    return (
        lax.div(tensor, 2),
        lax.rem(tensor, 2),
        lax.div(wide, NY),
        lax.rem(wide, NY),
    )


def device_of(x, core, z, y):
    return {"tensor": x * 2 + core, "wide": z * NY + y}


def wrap(value, size):
    return lax.rem(value + size, size)


def dot(left, right, left_dim, right_dim):
    return lax.dot_general(
        left, right, (((left_dim,), (right_dim,)), ((), ())), preferred_element_type=F32
    )


class Wire:
    def __init__(self, send_sem, recv_sem):
        self.send_sem, self.recv_sem = send_sem, recv_sem
        self.sent = []

    def make(self, number, source, target, device):
        return pltpu.make_async_remote_copy(
            src_ref=source,
            dst_ref=target,
            send_sem=self.send_sem.at[number],
            recv_sem=self.recv_sem.at[number],
            device_id=device,
            device_id_type=MESH,
        )

    def send(self, number, source, target, device):
        copy = self.make(number, source, target, device)
        copy.start()
        self.sent.append(copy)

    def arrived(self, number, landed, device):
        self.make(number, landed, landed, device).wait_recv()

    def drain(self):
        for copy in self.sent:
            copy.wait_send()


def slot_match(experts, rows, per_expert):
    row = lax.broadcasted_iota(jnp.int32, (rows, TOK), 0)
    expert, half, slot = row // per_expert, (row // 4) % 2, row % 4
    one, zero = jnp.ones((rows, TOK), F32), jnp.zeros((rows, TOK), F32)
    first = jnp.where(jnp.broadcast_to(experts[0:1], (rows, TOK)) == expert, one, zero)
    second = jnp.where(jnp.broadcast_to(experts[1:2], (rows, TOK)) == expert, one, zero)
    left = lax.broadcasted_iota(jnp.int32, (TOK, TOK), 0)
    right = lax.broadcasted_iota(jnp.int32, (TOK, TOK), 1)
    earlier = jnp.where(left < right, 1.0, 0.0).astype(F32)
    before = dot(first + second, earlier, 1, 0)
    at_slot = jnp.where(before == slot.astype(F32), one, zero)
    upper = jnp.where(half == 0, one, zero)
    return first * at_slot, second * at_slot, upper


def selection(wanted):
    column = lax.broadcasted_iota(jnp.int32, (128, 128), 1)
    return jnp.where(column == wanted, 1.0, 0.0).astype(BF)


class Gather:
    def __init__(self, wire, ref, base, place, swap, ring, sibling):
        self.wire, self.ref, self.base, self.swap, self.sibling = wire, ref, base, swap, sibling
        self.x, self.core, self.y = place
        self.up, self.down, self.fore, self.back = ring

    def at(self, a, b, ci, start=0, count=ROWS):
        dx, dy = (b, a) if self.swap else (a, b)
        xi, yi = wrap(self.x + dx, NX), wrap(self.y + dy, NY)
        return self.ref.at[
            pl.ds(pl.multiple_of(yi * ROWS + start, 32), count),
            pl.ds(pl.multiple_of((xi * 2 + ci) * FEAT, 128), FEAT),
        ]

    def push(self, number, piece, device):
        self.wire.send(self.base + number, piece, piece, device)

    def got(self, number, piece):
        self.wire.arrived(self.base + number, piece, self.sibling)

    def start(self):
        own = self.at(0, 0, self.core)
        self.push(0, own, self.up)
        self.push(1, own, self.down)

    def spread(self, k, a):
        own = self.at(a, 0, self.core)
        self.push(4 + 4 * k, own, self.fore)
        self.push(5 + 4 * k, own, self.back)
        self.push(20 + 4 * k, own, self.sibling)

    def first_near(self):
        self.got(0, self.at(-1, 0, self.core))
        self.push(2, self.at(-1, 0, self.core, 0, 32), self.up)
        self.spread(1, -1)
        self.got(1, self.at(1, 0, self.core))
        self.push(3, self.at(1, 0, self.core, 32, 32), self.down)
        self.spread(2, 1)

    def first_far(self):
        self.got(2, self.at(2, 0, self.core, 0, 32))
        self.got(3, self.at(2, 0, self.core, 32, 32))
        self.spread(3, 2)

    def second_near(self, k, a):
        self.got(4 + 4 * k, self.at(a, -1, self.core))
        self.push(6 + 4 * k, self.at(a, -1, self.core, 0, 32), self.fore)
        self.push(21 + 4 * k, self.at(a, -1, self.core), self.sibling)
        self.got(5 + 4 * k, self.at(a, 1, self.core))
        self.push(7 + 4 * k, self.at(a, 1, self.core, 32, 32), self.back)
        self.push(22 + 4 * k, self.at(a, 1, self.core), self.sibling)

    def second_far(self, k, a):
        self.got(6 + 4 * k, self.at(a, 2, self.core, 0, 32))
        self.got(7 + 4 * k, self.at(a, 2, self.core, 32, 32))
        self.push(23 + 4 * k, self.at(a, 2, self.core), self.sibling)

    def from_sibling(self):
        for k, a in enumerate((0, -1, 1, 2)):
            for m, b in enumerate((0, -1, 1, 2)):
                self.got(20 + 4 * k + m, self.at(a, b, 1 - self.core))


class Scatter:
    def __init__(self, wire, base, buffers, a, b, first_peers, second_peers):
        self.wire, self.base = wire, base
        self.acc, self.near, self.full, self.mid, self.last = buffers
        self.a, self.b = a, b
        self.first_peers, self.second_peers = first_peers, second_peers

    def far(self):
        far = wrap(self.a + 2, 4)
        for side, peer in ((0, 0), (1, 2)):
            self.wire.send(
                self.base + side,
                self.acc.at[far, pl.ds(2 * side, 2)],
                self.near.at[side],
                self.first_peers[peer],
            )

    def close(self):
        for side, chunk, peer in ((0, 1, 0), (1, 3, 2)):
            self.wire.arrived(self.base + side, self.near.at[side], self.first_peers[peer])
            there = wrap(self.a + chunk, 4)
            for i in range(2):
                self.acc[there, 2 * side + i] = (
                    self.acc[there, 2 * side + i].astype(F32) + self.near[side, i].astype(F32)
                ).astype(BF)
            self.wire.send(
                self.base + 2 + side,
                self.acc.at[there],
                self.full.at[side],
                self.first_peers[peer],
            )

    def across(self):
        for side in range(2):
            self.wire.arrived(self.base + 2 + side, self.full.at[side], self.first_peers[0])
        for i in range(4):
            self.mid[i] = (
                self.acc[self.a, i].astype(F32)
                + self.full[0, i].astype(F32)
                + self.full[1, i].astype(F32)
            ).astype(BF)
        for d in range(1, 4):
            self.wire.send(
                self.base + 3 + d,
                self.mid.at[wrap(self.b + d, 4)],
                self.last.at[d - 1],
                self.second_peers[d - 1],
            )

    def total(self):
        result = self.mid[self.b].astype(F32)
        for d in range(1, 4):
            self.wire.arrived(self.base + 3 + d, self.last.at[d - 1], self.second_peers[0])
            result = result + self.last[d - 1].astype(F32)
        return result


def layer_kernel(
    tokens_hbm,
    cotangent_hbm,
    gates_hbm,
    experts_hbm,
    wg_hbm,
    wu_hbm,
    wd_hbm,
    grad_ref,
    routing_ref,
    dwg_hbm,
    dwu_hbm,
    dwd_hbm,
    tokens_ref,
    cotangent_ref,
    gates_ref,
    experts_ref,
    wg_ref,
    wu_ref,
    wd_ref,
    dwg_ref,
    dwu_ref,
    dwd_ref,
    load_sem,
    out_buf,
    in_buf,
    x_ref,
    c_ref,
    sums,
    gg_ref,
    gu_ref,
    hid_ref,
    r_out,
    r_in,
    acc_p,
    acc_q,
    near_p,
    near_q,
    full_p,
    full_q,
    mid_p,
    mid_q,
    last_p,
    last_q,
    t_ref,
    t_y,
    t_sum,
    t_t,
    back_out,
    back_in,
    send_sem,
    recv_sem,
):
    x, core, z, y = position()
    tensor = x * 2 + core
    small = [
        pltpu.make_async_copy(source, target, load_sem.at[i])
        for i, (source, target) in enumerate(
            (
                (experts_hbm, experts_ref),
                (gates_hbm, gates_ref),
                (tokens_hbm, tokens_ref),
                (cotangent_hbm, cotangent_ref),
            )
        )
    ]
    weights = [
        pltpu.make_async_copy(source, target, load_sem.at[4 + i])
        for i, (source, target) in enumerate(
            ((wg_hbm, wg_ref), (wu_hbm, wu_ref), (wd_hbm, wd_ref))
        )
    ]
    for copy in small:
        copy.start()
    peers_z = [device_of(x, core, wrap(z + d, NZ), y) for d in range(1, NZ)]
    peers_t = [{"tensor": wrap(tensor + d, 8), "wide": z * NY + y} for d in range(1, 8)]
    peers_y = [device_of(x, core, z, wrap(y + d, NY)) for d in range(1, NY)]
    peers_x = [device_of(wrap(x + d, NX), core, z, y) for d in range(1, NX)]
    sibling = device_of(x, 1 - core, z, y)

    barrier = pltpu.get_barrier_semaphore()
    partners = [peers_z[d - 1] for d in Z_ORDER] + peers_y + peers_t
    for partner in partners:
        pl.semaphore_signal(barrier, inc=1, device_id=partner, device_id_type=MESH)
    for copy in weights:
        copy.start()
    for copy in small:
        copy.wait()

    first, second, upper = slot_match(experts_ref[...], 64, 8)
    gates = gates_ref[...].astype(F32)
    pick_in = ((first + second) * upper).astype(BF)
    pick_up = ((first * gates[0:1] + second * gates[1:2]) * (1.0 - upper)).astype(BF)
    chosen = dot(pick_in, tokens_ref[...], 1, 0) + dot(pick_up, cotangent_ref[...], 1, 0)
    out_buf[...] = chosen.reshape(8, 8, FEAT).astype(BF)
    pl.semaphore_wait(barrier, len(partners))

    wire = Wire(send_sem, recv_sem)
    for d in Z_ORDER:
        there = wrap(z + d, NZ)
        wire.send(d - 1, out_buf.at[lax.div(there, 2)], in_buf.at[z], peers_z[d - 1])
    in_buf[z] = out_buf[lax.div(z, 2)]
    for d in Z_ORDER[::-1]:
        wire.arrived(d - 1, in_buf.at[wrap(z - d, NZ)], sibling)

    out_row = lax.broadcasted_iota(jnp.int32, (128, 128), 0)
    order = selection((out_row % 64) // 4 * 8 + out_row // 64 * 4 + out_row % 4)
    came = in_buf[...].astype(F32).reshape(128, FEAT).astype(BF)
    arranged = dot(order, came, 1, 0).astype(BF)
    my_rows = pl.ds(pl.multiple_of(y * ROWS, ROWS), ROWS)
    my_columns = pl.ds(pl.multiple_of(tensor * FEAT, 128), FEAT)
    x_ref[my_rows, my_columns] = arranged[0:64]
    c_ref[my_rows, my_columns] = arranged[64:128]

    on_x, on_y = [peers_x[0], peers_x[2]], [peers_y[0], peers_y[2]]
    place = (x, core, y)
    gathers = (
        Gather(wire, x_ref, 15, place, False, on_x + on_y, sibling),
        Gather(wire, c_ref, 51, place, True, on_y + on_x, sibling),
    )
    for one in gathers:
        one.start()
    for one in gathers:
        one.spread(0, 0)
    for one in gathers:
        one.first_near()
    for one in gathers:
        one.second_near(0, 0)
    for one in gathers:
        one.first_far()
    for k, a in ((1, -1), (2, 1)):
        for one in gathers:
            one.second_near(k, a)
        for one in gathers:
            one.second_far(k - 1, (0, -1)[k - 1])
    for one in gathers:
        one.second_near(3, 2)
    for one in gathers:
        one.second_far(2, 1)
    for one in gathers:
        one.second_far(3, 2)

    def columns_of(xi, ci):
        return pl.ds(pl.multiple_of((xi * 2 + ci) * FEAT, 128), FEAT)

    def forward(ci):
        gate = up = through = None
        for xi in range(NX):
            columns = columns_of(xi, ci)
            terms = (
                dot(x_ref[:, columns], wg_ref[0, columns, :], 1, 0),
                dot(x_ref[:, columns], wu_ref[0, columns, :], 1, 0),
                dot(c_ref[:, columns], wd_ref[0, :, columns], 1, 1),
            )
            if gate is None:
                gate, up, through = terms
            else:
                gate, up, through = gate + terms[0], up + terms[1], through + terms[2]
        return gate, up, through

    for copy in weights:
        copy.wait()
    sums[0], sums[1], sums[2] = forward(core)
    for one in gathers:
        one.from_sibling()
    pre_gate, pre_up, hidden_grad = forward(1 - core)
    pre_gate, pre_up, hidden_grad = pre_gate + sums[0], pre_up + sums[1], hidden_grad + sums[2]
    sig = jax.nn.sigmoid(pre_gate)
    act = pre_gate * sig
    hidden = act * pre_up
    gg_ref[...] = (hidden_grad * pre_up * sig * (1.0 + pre_gate * (1.0 - sig))).astype(BF)
    gu_ref[...] = (hidden_grad * act).astype(BF)
    hid_ref[...] = hidden.astype(BF)
    row = lax.broadcasted_iota(jnp.int32, (ROWS, 128), 0)
    lane = lax.broadcasted_iota(jnp.int32, (ROWS, 128), 1)
    row_sums = jnp.sum(hidden_grad * hidden, axis=1, keepdims=True)
    for yi in range(NY):
        part = jnp.broadcast_to(row_sums[yi * ROWS : (yi + 1) * ROWS], (ROWS, 128))
        line = jnp.sum(jnp.where(row == lane, part, 0.0), axis=0, keepdims=True)
        t_ref[yi] = jnp.broadcast_to(line, (8, 128))
    for d in range(1, NY):
        wire.send(86 + d, t_ref.at[wrap(y + d, NY)], t_y.at[d - 1], peers_y[d - 1])

    def returned(xi, ci):
        columns = columns_of(xi, ci)
        return dot(gg_ref[...], wg_ref[0, columns, :], 1, 1) + dot(
            gu_ref[...], wu_ref[0, columns, :], 1, 1
        )

    x_order = (2, 1, 3, 0)
    for k, d in enumerate(x_order):
        r_out[k] = returned(wrap(x + d, NX), 1 - core).astype(BF)
        wire.send(90 + k, r_out.at[k], r_in.at[k], sibling)
    for k, d in enumerate(x_order):
        xi = wrap(x + d, NX)
        own = returned(xi, core)
        wire.arrived(90 + k, r_in.at[k], sibling)
        total = (own + r_in[k].astype(F32)).astype(BF)
        for yi in range(NY):
            acc_p[xi, yi] = total[yi * ROWS : yi * ROWS + 32]
            acc_q[yi, xi] = total[yi * ROWS + 32 : yi * ROWS + 64]

    def weight_grads(which):
        step = 512
        for k in range(D // step):
            rows = pl.ds(k * step, step)
            if which == 0:
                dwd_ref[0, :, rows] = dot(hid_ref[...], c_ref[:, rows], 0, 0).astype(BF)
            if which == 1:
                dwg_ref[0, rows, :] = dot(x_ref[:, rows], gg_ref[...], 0, 0).astype(BF)
            if which == 2:
                dwu_ref[0, rows, :] = dot(x_ref[:, rows], gu_ref[...], 0, 0).astype(BF)

    stores = [
        pltpu.make_async_copy(source, target, load_sem.at[7 + i])
        for i, (source, target) in enumerate(
            ((dwd_ref, dwd_hbm), (dwg_ref, dwg_hbm), (dwu_ref, dwu_hbm))
        )
    ]
    scatters = (
        Scatter(
            wire, 94, (acc_p, near_p, full_p, mid_p, last_p), x, y, peers_x, peers_y
        ),
        Scatter(
            wire, 101, (acc_q, near_q, full_q, mid_q, last_q), y, x, peers_y, peers_x
        ),
    )
    for one in scatters:
        one.far()
    line = t_ref[y]
    for d in range(1, NY):
        wire.arrived(86 + d, t_y.at[d - 1], sibling)
        line = line + t_y[d - 1]
    t_sum[...] = line
    t_t[tensor] = line
    for d in range(1, 8):
        wire.send(107 + d, t_sum, t_t.at[tensor], peers_t[d - 1])
    weight_grads(0)
    stores[0].start()
    for one in scatters:
        one.close()
    weight_grads(1)
    stores[1].start()
    for one in scatters:
        one.across()
    for d in range(1, 8):
        wire.arrived(107 + d, t_t.at[wrap(tensor - d, 8)], sibling)
    line = t_t[0]
    for i in range(1, 8):
        line = line + t_t[i]
    spread = jnp.where(row == lane, jnp.broadcast_to(line[0:1], (ROWS, 128)), 0.0)
    column = jnp.broadcast_to(jnp.sum(spread, axis=1, keepdims=True), (ROWS, 128))
    result = jnp.concatenate([one.total() for one in scatters], axis=0)
    pair = jnp.concatenate(
        [
            result[:, 0:256],
            jnp.concatenate([result[:, 256:FEAT], column], axis=1),
        ],
        axis=0,
    ).astype(BF)
    order = selection((out_row // 4) % 2 * 64 + out_row // 8 * 4 + out_row % 4)
    back_out[...] = dot(order, pair, 1, 0).reshape(NZ, 8, 256).astype(BF)
    for d in Z_ORDER:
        wire.send(114 + d, back_out.at[wrap(z + d, NZ)], back_in.at[z], peers_z[d - 1])
    back_in[z] = back_out[z]
    weight_grads(2)
    stores[2].start()

    first, second, upper = slot_match(experts_ref[...], 128, 16)
    lower = 1.0 - upper
    pick_head = ((first + second) * upper).astype(BF)
    pick_tail = ((first + second) * lower).astype(BF)
    pick_first = (first * lower).astype(BF)
    pick_second = (second * lower).astype(BF)
    for d in Z_ORDER[::-1]:
        wire.arrived(114 + d, back_in.at[wrap(z - d, NZ)], sibling)
    came = back_in[...].astype(F32).reshape(128, 256).astype(BF)
    grad_ref[:, 0:256] = dot(pick_head, came, 0, 0).astype(BF)
    grad_ref[:, 256:FEAT] = dot(pick_tail, came[:, 0:128], 0, 0).astype(BF)
    at_first = dot(came[:, 128:], pick_first, 0, 0)
    at_second = dot(came[:, 128:], pick_second, 0, 0)
    routing_ref[0:1, :] = at_first[0:1, :] / gates[0:1]
    routing_ref[1:2, :] = at_second[0:1, :] / gates[1:2]
    for copy in stores:
        copy.wait()
    wire.drain()


def layer(*arguments):
    quarter = [pltpu.VMEM((4, 4, 32, FEAT), BF)] * 2
    near = [pltpu.VMEM((2, 2, 32, FEAT), BF)] * 2
    full = [pltpu.VMEM((2, 4, 32, FEAT), BF)] * 2
    mid = [pltpu.VMEM((4, 32, FEAT), BF)] * 2
    last = [pltpu.VMEM((3, 32, FEAT), BF)] * 2
    return pl.pallas_call(
        layer_kernel,
        name="layer",
        out_shape=(
            jax.ShapeDtypeStruct((TOK, FEAT), BF),
            jax.ShapeDtypeStruct((2, TOK), F32),
            jax.ShapeDtypeStruct((1, D, HID), BF),
            jax.ShapeDtypeStruct((1, D, HID), BF),
            jax.ShapeDtypeStruct((1, HID, D), BF),
        ),
        in_specs=[HBM] * 7,
        out_specs=(VMEM, VMEM, HBM, HBM, HBM),
        scratch_shapes=[
            pltpu.VMEM((TOK, FEAT), BF),
            pltpu.VMEM((TOK, FEAT), BF),
            pltpu.VMEM((2, TOK), BF),
            pltpu.VMEM((2, TOK), jnp.int32),
            pltpu.VMEM((1, D, HID), BF),
            pltpu.VMEM((1, D, HID), BF),
            pltpu.VMEM((1, HID, D), BF),
            pltpu.VMEM((1, D, HID), BF),
            pltpu.VMEM((1, D, HID), BF),
            pltpu.VMEM((1, HID, D), BF),
            pltpu.SemaphoreType.DMA((10,)),
            pltpu.VMEM((8, 8, FEAT), BF),
            pltpu.VMEM((NZ, 8, FEAT), BF),
            pltpu.VMEM((SLOTS, D), BF),
            pltpu.VMEM((SLOTS, D), BF),
            pltpu.VMEM((3, SLOTS, HID), F32),
            pltpu.VMEM((SLOTS, HID), BF),
            pltpu.VMEM((SLOTS, HID), BF),
            pltpu.VMEM((SLOTS, HID), BF),
            pltpu.VMEM((NX, SLOTS, FEAT), BF),
            pltpu.VMEM((NX, SLOTS, FEAT), BF),
            *quarter,
            *near,
            *full,
            *mid,
            *last,
            pltpu.VMEM((NY, 8, 128), F32),
            pltpu.VMEM((3, 8, 128), F32),
            pltpu.VMEM((8, 128), F32),
            pltpu.VMEM((8, 8, 128), F32),
            pltpu.VMEM((NZ, 8, 256), BF),
            pltpu.VMEM((NZ, 8, 256), BF),
            pltpu.SemaphoreType.DMA((130,)),
            pltpu.SemaphoreType.DMA((130,)),
        ],
        compiler_params=pltpu.CompilerParams(
            collective_id=0, has_side_effects=True, vmem_limit_bytes=60 << 20
        ),
    )(*arguments)


def emit_kernel(*refs):
    sources, targets, stage, load_sem, store_sem = refs[:5], refs[5:10], refs[10:15], refs[15], refs[16]
    pieces = [(i, None) for i in range(2)]
    pieces += [(i, part) for part in range(2) for i in range(2, 5)]

    def view(ref, part):
        if part is None:
            return ref
        half = ref.shape[1] // 2
        return ref.at[:, pl.ds(part * half, half)]

    loads = [
        pltpu.make_async_copy(view(sources[i], part), view(stage[i], part), load_sem.at[n])
        for n, (i, part) in enumerate(pieces)
    ]
    stores = [
        pltpu.make_async_copy(view(stage[i], part), view(targets[i], part), store_sem.at[n])
        for n, (i, part) in enumerate(pieces)
    ]
    for copy in loads:
        copy.start()
    for load, store in zip(loads, stores):
        load.wait()
        store.start()
    for copy in stores:
        copy.wait()


def emit(*results):
    return pl.pallas_call(
        emit_kernel,
        name="emit",
        out_shape=tuple(jax.ShapeDtypeStruct(one.shape, one.dtype) for one in results),
        in_specs=[HBM] * 5,
        out_specs=(HBM,) * 5,
        scratch_shapes=[
            *[pltpu.VMEM(one.shape, one.dtype) for one in results],
            pltpu.SemaphoreType.DMA((8,)),
            pltpu.SemaphoreType.DMA((8,)),
        ],
        compiler_params=pltpu.CompilerParams(vmem_limit_bytes=60 << 20),
    )(*results)


def shards(tokens, cotangent, gates, experts, w_gate, w_up, w_down):
    results = layer(tokens, cotangent, gates.T, experts.T, w_gate, w_up, w_down)
    input_grad, routing_grad, gate_grad, up_grad, down_grad = emit(*results)
    return input_grad, routing_grad.T, gate_grad, up_grad, down_grad


def solution(mesh):
    return jax.shard_map(
        shards,
        mesh=mesh,
        in_specs=(
            P("wide", "tensor"),
            P("wide", "tensor"),
            P("wide", None),
            P("wide", None),
            P("wide", None, "tensor"),
            P("wide", None, "tensor"),
            P("wide", "tensor", None),
        ),
        out_specs=(
            P("wide", "tensor"),
            P("wide", None),
            P("wide", None, "tensor"),
            P("wide", None, "tensor"),
            P("wide", "tensor", None),
        ),
        check_vma=False,
    )
```

```python
import jax
import jax.numpy as jnp
from jax import lax
from jax.experimental import pallas as pl
from jax.experimental.pallas import tpu as pltpu
from jax.sharding import PartitionSpec as P

MESH = pl.DeviceIdType.MESH
NZ, NY, NX = 16, 4, 4
TOK = 8
D = 3072
FEAT = 384
HID = 128
ROWS = 64
SLOTS = 256
BF = jnp.bfloat16
F32 = jnp.float32
VMEM = pl.BlockSpec(memory_space=pltpu.VMEM)
HBM = pl.BlockSpec(memory_space=pltpu.MemorySpace.HBM)
Z_ORDER = (8, 7, 9, 6, 10, 5, 11, 4, 12, 3, 13, 2, 14, 1, 15)


def position():
    tensor, wide = lax.axis_index("tensor"), lax.axis_index("wide")
    return (
        lax.div(tensor, 2),
        lax.rem(tensor, 2),
        lax.div(wide, NY),
        lax.rem(wide, NY),
    )


def device_of(x, core, z, y):
    return {"tensor": x * 2 + core, "wide": z * NY + y}


def wrap(value, size):
    return lax.rem(value + size, size)


def dot(left, right, left_dim, right_dim):
    return lax.dot_general(
        left, right, (((left_dim,), (right_dim,)), ((), ())), preferred_element_type=F32
    )


class Wire:
    def __init__(self, send_sem, recv_sem):
        self.send_sem, self.recv_sem = send_sem, recv_sem
        self.sent = []

    def make(self, number, source, target, device):
        return pltpu.make_async_remote_copy(
            src_ref=source,
            dst_ref=target,
            send_sem=self.send_sem.at[number],
            recv_sem=self.recv_sem.at[number],
            device_id=device,
            device_id_type=MESH,
        )

    def send(self, number, source, target, device):
        copy = self.make(number, source, target, device)
        copy.start()
        self.sent.append(copy)

    def arrived(self, number, landed, device):
        self.make(number, landed, landed, device).wait_recv()

    def drain(self):
        for copy in self.sent:
            copy.wait_send()


def slot_match(experts, rows, per_expert):
    row = lax.broadcasted_iota(jnp.int32, (rows, TOK), 0)
    expert, half, slot = row // per_expert, (row // 4) % 2, row % 4
    one, zero = jnp.ones((rows, TOK), F32), jnp.zeros((rows, TOK), F32)
    first = jnp.where(jnp.broadcast_to(experts[0:1], (rows, TOK)) == expert, one, zero)
    second = jnp.where(jnp.broadcast_to(experts[1:2], (rows, TOK)) == expert, one, zero)
    left = lax.broadcasted_iota(jnp.int32, (TOK, TOK), 0)
    right = lax.broadcasted_iota(jnp.int32, (TOK, TOK), 1)
    earlier = jnp.where(left < right, 1.0, 0.0).astype(F32)
    before = dot(first + second, earlier, 1, 0)
    at_slot = jnp.where(before == slot.astype(F32), one, zero)
    upper = jnp.where(half == 0, one, zero)
    return first * at_slot, second * at_slot, upper


def selection(wanted):
    column = lax.broadcasted_iota(jnp.int32, (128, 128), 1)
    return jnp.where(column == wanted, 1.0, 0.0).astype(BF)


class Gather:
    def __init__(self, wire, ref, base, place, swap, first_peers, second_peers, sibling):
        self.wire, self.ref, self.base, self.swap, self.sibling = wire, ref, base, swap, sibling
        self.x, self.core, self.y = place
        self.first_peers, self.second_peers = first_peers, second_peers

    def at(self, a, b, ci):
        dx, dy = (b, a) if self.swap else (a, b)
        xi, yi = wrap(self.x - dx, NX), wrap(self.y - dy, NY)
        return self.ref.at[
            pl.ds(pl.multiple_of(yi * ROWS, ROWS), ROWS),
            pl.ds(pl.multiple_of((xi * 2 + ci) * FEAT, 128), FEAT),
        ]

    def push(self, number, piece, device):
        self.wire.send(self.base + number, piece, piece, device)

    def got(self, number, piece):
        self.wire.arrived(self.base + number, piece, self.sibling)

    def start(self):
        for d in (2, 1, 3):
            self.push(d - 1, self.at(0, 0, self.core), self.first_peers[d - 1])

    def spread(self, k):
        block = self.at(k, 0, self.core)
        if k:
            self.got(k - 1, block)
        for d in (2, 1, 3):
            self.push(3 * k + 2 + d, block, self.second_peers[d - 1])

    def feed(self, k, m):
        block = self.at(k, m, self.core)
        if m:
            self.got(3 * k + 2 + m, block)
        self.push(15 + 4 * k + m, block, self.sibling)

    def from_sibling(self):
        for k in range(4):
            for m in range(4):
                self.got(15 + 4 * k + m, self.at(k, m, 1 - self.core))


class Scatter:
    def __init__(self, wire, base, buffers, a, b, first_peers, second_peers):
        self.wire, self.base = wire, base
        self.acc, self.full, self.mid, self.last = buffers
        self.a, self.b = a, b
        self.first_peers, self.second_peers = first_peers, second_peers

    def send(self, d):
        self.wire.send(
            self.base + d - 1,
            self.acc.at[wrap(self.a + d, 4)],
            self.full.at[d - 1],
            self.first_peers[d - 1],
        )

    def across(self):
        for d in (1, 3, 2):
            self.wire.arrived(self.base + d - 1, self.full.at[d - 1], self.first_peers[0])
        for d in (2, 1, 3, 0):
            i = wrap(self.b + d, 4)
            total = self.acc[self.a, i].astype(F32)
            for e in range(3):
                total = total + self.full[e, i].astype(F32)
            self.mid[i] = total.astype(BF)
            if d:
                self.wire.send(
                    self.base + 2 + d,
                    self.mid.at[i],
                    self.last.at[d - 1],
                    self.second_peers[d - 1],
                )

    def total(self):
        result = self.mid[self.b].astype(F32)
        for d in range(1, 4):
            self.wire.arrived(self.base + 2 + d, self.last.at[d - 1], self.second_peers[0])
            result = result + self.last[d - 1].astype(F32)
        return result


def layer_kernel(
    tokens_hbm,
    cotangent_hbm,
    gates_hbm,
    experts_hbm,
    wg_hbm,
    wu_hbm,
    wd_hbm,
    grad_ref,
    routing_ref,
    dwg_hbm,
    dwu_hbm,
    dwd_hbm,
    tokens_ref,
    cotangent_ref,
    gates_ref,
    experts_ref,
    wg_ref,
    wu_ref,
    wd_ref,
    dwg_ref,
    dwu_ref,
    dwd_ref,
    load_sem,
    out_buf,
    in_buf,
    x_ref,
    c_ref,
    sums,
    gg_ref,
    gu_ref,
    hid_ref,
    r_out,
    r_in,
    acc_p,
    acc_q,
    full_p,
    full_q,
    mid_p,
    mid_q,
    last_p,
    last_q,
    t_ref,
    t_y,
    t_sum,
    t_t,
    back_out,
    back_in,
    send_sem,
    recv_sem,
):
    x, core, z, y = position()
    tensor = x * 2 + core
    small = [
        pltpu.make_async_copy(source, target, load_sem.at[i])
        for i, (source, target) in enumerate(
            (
                (experts_hbm, experts_ref),
                (gates_hbm, gates_ref),
                (tokens_hbm, tokens_ref),
                (cotangent_hbm, cotangent_ref),
            )
        )
    ]
    weights = [
        pltpu.make_async_copy(source, target, load_sem.at[4 + i])
        for i, (source, target) in enumerate(
            ((wg_hbm, wg_ref), (wu_hbm, wu_ref), (wd_hbm, wd_ref))
        )
    ]
    for copy in small:
        copy.start()
    peers_z = [device_of(x, core, wrap(z + d, NZ), y) for d in range(1, NZ)]
    peers_t = [{"tensor": wrap(tensor + d, 8), "wide": z * NY + y} for d in range(1, 8)]
    peers_y = [device_of(x, core, z, wrap(y + d, NY)) for d in range(1, NY)]
    peers_x = [device_of(wrap(x + d, NX), core, z, y) for d in range(1, NX)]
    sibling = device_of(x, 1 - core, z, y)

    barrier = pltpu.get_barrier_semaphore()
    partners = [peers_z[d - 1] for d in Z_ORDER] + peers_y + peers_t
    for partner in partners:
        pl.semaphore_signal(barrier, inc=1, device_id=partner, device_id_type=MESH)
    for copy in weights:
        copy.start()
    for copy in small:
        copy.wait()

    first, second, upper = slot_match(experts_ref[...], 64, 8)
    gates = gates_ref[...].astype(F32)
    pick_in = ((first + second) * upper).astype(BF)
    pick_up = ((first * gates[0:1] + second * gates[1:2]) * (1.0 - upper)).astype(BF)
    chosen = dot(pick_in, tokens_ref[...], 1, 0) + dot(pick_up, cotangent_ref[...], 1, 0)
    out_buf[...] = chosen.reshape(8, 8, FEAT).astype(BF)
    pl.semaphore_wait(barrier, len(partners))

    wire = Wire(send_sem, recv_sem)
    for d in Z_ORDER:
        there = wrap(z + d, NZ)
        wire.send(d - 1, out_buf.at[lax.div(there, 2)], in_buf.at[z], peers_z[d - 1])
    in_buf[z] = out_buf[lax.div(z, 2)]
    for d in Z_ORDER[::-1]:
        wire.arrived(d - 1, in_buf.at[wrap(z - d, NZ)], sibling)

    out_row = lax.broadcasted_iota(jnp.int32, (128, 128), 0)
    order = selection((out_row % 64) // 4 * 8 + out_row // 64 * 4 + out_row % 4)
    came = in_buf[...].astype(F32).reshape(128, FEAT).astype(BF)
    arranged = dot(order, came, 1, 0).astype(BF)
    my_rows = pl.ds(pl.multiple_of(y * ROWS, ROWS), ROWS)
    my_columns = pl.ds(pl.multiple_of(tensor * FEAT, 128), FEAT)
    x_ref[my_rows, my_columns] = arranged[0:64]
    c_ref[my_rows, my_columns] = arranged[64:128]

    place = (x, core, y)
    gathers = (
        Gather(wire, x_ref, 15, place, False, peers_x, peers_y, sibling),
        Gather(wire, c_ref, 46, place, True, peers_y, peers_x, sibling),
    )
    for one in gathers:
        one.start()
    for one in gathers:
        one.spread(0)
    for k in (1, 3, 2):
        for one in gathers:
            one.spread(k)
    for k in (0, 1, 3, 2):
        for m in (0, 1, 3, 2):
            for one in gathers:
                one.feed(k, m)

    def columns_of(xi, ci):
        return pl.ds(pl.multiple_of((xi * 2 + ci) * FEAT, 128), FEAT)

    def forward(ci):
        gate = up = through = None
        for xi in range(NX):
            columns = columns_of(xi, ci)
            terms = (
                dot(x_ref[:, columns], wg_ref[0, columns, :], 1, 0),
                dot(x_ref[:, columns], wu_ref[0, columns, :], 1, 0),
                dot(c_ref[:, columns], wd_ref[0, :, columns], 1, 1),
            )
            if gate is None:
                gate, up, through = terms
            else:
                gate, up, through = gate + terms[0], up + terms[1], through + terms[2]
        return gate, up, through

    for copy in weights:
        copy.wait()
    sums[0], sums[1], sums[2] = forward(core)
    for one in gathers:
        one.from_sibling()
    pre_gate, pre_up, hidden_grad = forward(1 - core)
    pre_gate, pre_up, hidden_grad = pre_gate + sums[0], pre_up + sums[1], hidden_grad + sums[2]
    sig = jax.nn.sigmoid(pre_gate)
    act = pre_gate * sig
    hidden = act * pre_up
    gg_ref[...] = (hidden_grad * pre_up * sig * (1.0 + pre_gate * (1.0 - sig))).astype(BF)
    gu_ref[...] = (hidden_grad * act).astype(BF)

    def returned(xi, ci):
        columns = columns_of(xi, ci)
        return dot(gg_ref[...], wg_ref[0, columns, :], 1, 1) + dot(
            gu_ref[...], wu_ref[0, columns, :], 1, 1
        )

    scatters = (
        Scatter(wire, 94, (acc_p, full_p, mid_p, last_p), x, y, peers_x, peers_y),
        Scatter(wire, 101, (acc_q, full_q, mid_q, last_q), y, x, peers_y, peers_x),
    )
    x_order = (2, 1, 3, 0)
    for k, d in enumerate(x_order):
        r_out[k] = returned(wrap(x + d, NX), 1 - core).astype(BF)
        wire.send(90 + k, r_out.at[k], r_in.at[k], sibling)
    hid_ref[...] = hidden.astype(BF)
    row = lax.broadcasted_iota(jnp.int32, (ROWS, 128), 0)
    lane = lax.broadcasted_iota(jnp.int32, (ROWS, 128), 1)
    row_sums = jnp.sum(hidden_grad * hidden, axis=1, keepdims=True)
    for yi in range(NY):
        part = jnp.broadcast_to(row_sums[yi * ROWS : (yi + 1) * ROWS], (ROWS, 128))
        line = jnp.sum(jnp.where(row == lane, part, 0.0), axis=0, keepdims=True)
        t_ref[yi] = jnp.broadcast_to(line, (8, 128))
    for d in range(1, NY):
        wire.send(86 + d, t_ref.at[wrap(y + d, NY)], t_y.at[d - 1], peers_y[d - 1])
    for k, d in enumerate(x_order):
        xi = wrap(x + d, NX)
        own = returned(xi, core)
        wire.arrived(90 + k, r_in.at[k], sibling)
        total = (own + r_in[k].astype(F32)).astype(BF)
        for yi in range(NY):
            acc_p[xi, yi] = total[yi * ROWS : yi * ROWS + 32]
            acc_q[yi, xi] = total[yi * ROWS + 32 : yi * ROWS + 64]
        if d:
            scatters[0].send(d)
    for d in (2, 1, 3):
        scatters[1].send(d)

    def weight_grads(which):
        step = 512
        for k in range(D // step):
            rows = pl.ds(k * step, step)
            if which == 0:
                dwd_ref[0, :, rows] = dot(hid_ref[...], c_ref[:, rows], 0, 0).astype(BF)
            if which == 1:
                dwg_ref[0, rows, :] = dot(x_ref[:, rows], gg_ref[...], 0, 0).astype(BF)
            if which == 2:
                dwu_ref[0, rows, :] = dot(x_ref[:, rows], gu_ref[...], 0, 0).astype(BF)

    stores = [
        pltpu.make_async_copy(source, target, load_sem.at[7 + i])
        for i, (source, target) in enumerate(
            ((dwd_ref, dwd_hbm), (dwg_ref, dwg_hbm), (dwu_ref, dwu_hbm))
        )
    ]
    line = t_ref[y]
    for d in range(1, NY):
        wire.arrived(86 + d, t_y.at[d - 1], sibling)
        line = line + t_y[d - 1]
    t_sum[...] = line
    t_t[tensor] = line
    for d in range(1, 8):
        wire.send(107 + d, t_sum, t_t.at[tensor], peers_t[d - 1])
    weight_grads(0)
    stores[0].start()
    weight_grads(1)
    stores[1].start()
    for one in scatters:
        one.across()
    weight_grads(2)
    stores[2].start()
    for d in range(1, 8):
        wire.arrived(107 + d, t_t.at[wrap(tensor - d, 8)], sibling)
    line = t_t[0]
    for i in range(1, 8):
        line = line + t_t[i]
    spread = jnp.where(row == lane, jnp.broadcast_to(line[0:1], (ROWS, 128)), 0.0)
    column = jnp.broadcast_to(jnp.sum(spread, axis=1, keepdims=True), (ROWS, 128))
    result = jnp.concatenate([one.total() for one in scatters], axis=0)
    pair = jnp.concatenate(
        [
            result[:, 0:256],
            jnp.concatenate([result[:, 256:FEAT], column], axis=1),
        ],
        axis=0,
    ).astype(BF)
    order = selection((out_row // 4) % 2 * 64 + out_row // 8 * 4 + out_row % 4)
    back_out[...] = dot(order, pair, 1, 0).reshape(NZ, 8, 256).astype(BF)
    for d in Z_ORDER:
        wire.send(114 + d, back_out.at[wrap(z + d, NZ)], back_in.at[z], peers_z[d - 1])
    back_in[z] = back_out[z]

    first, second, upper = slot_match(experts_ref[...], 128, 16)
    lower = 1.0 - upper
    pick_head = ((first + second) * upper).astype(BF)
    pick_tail = ((first + second) * lower).astype(BF)
    pick_first = (first * lower).astype(BF)
    pick_second = (second * lower).astype(BF)
    for d in Z_ORDER[::-1]:
        wire.arrived(114 + d, back_in.at[wrap(z - d, NZ)], sibling)
    came = back_in[...].astype(F32).reshape(128, 256).astype(BF)
    grad_ref[:, 0:256] = dot(pick_head, came, 0, 0).astype(BF)
    grad_ref[:, 256:FEAT] = dot(pick_tail, came[:, 0:128], 0, 0).astype(BF)
    at_first = dot(came[:, 128:], pick_first, 0, 0)
    at_second = dot(came[:, 128:], pick_second, 0, 0)
    routing_ref[0:1, :] = at_first[0:1, :] / gates[0:1]
    routing_ref[1:2, :] = at_second[0:1, :] / gates[1:2]
    for copy in stores:
        copy.wait()
    wire.drain()


def layer(*arguments):
    quarter = [pltpu.VMEM((4, 4, 32, FEAT), BF)] * 2
    full = [pltpu.VMEM((3, 4, 32, FEAT), BF)] * 2
    mid = [pltpu.VMEM((4, 32, FEAT), BF)] * 2
    last = [pltpu.VMEM((3, 32, FEAT), BF)] * 2
    return pl.pallas_call(
        layer_kernel,
        name="layer",
        out_shape=(
            jax.ShapeDtypeStruct((TOK, FEAT), BF),
            jax.ShapeDtypeStruct((2, TOK), F32),
            jax.ShapeDtypeStruct((1, D, HID), BF),
            jax.ShapeDtypeStruct((1, D, HID), BF),
            jax.ShapeDtypeStruct((1, HID, D), BF),
        ),
        in_specs=[HBM] * 7,
        out_specs=(VMEM, VMEM, HBM, HBM, HBM),
        scratch_shapes=[
            pltpu.VMEM((TOK, FEAT), BF),
            pltpu.VMEM((TOK, FEAT), BF),
            pltpu.VMEM((2, TOK), BF),
            pltpu.VMEM((2, TOK), jnp.int32),
            pltpu.VMEM((1, D, HID), BF),
            pltpu.VMEM((1, D, HID), BF),
            pltpu.VMEM((1, HID, D), BF),
            pltpu.VMEM((1, D, HID), BF),
            pltpu.VMEM((1, D, HID), BF),
            pltpu.VMEM((1, HID, D), BF),
            pltpu.SemaphoreType.DMA((10,)),
            pltpu.VMEM((8, 8, FEAT), BF),
            pltpu.VMEM((NZ, 8, FEAT), BF),
            pltpu.VMEM((SLOTS, D), BF),
            pltpu.VMEM((SLOTS, D), BF),
            pltpu.VMEM((3, SLOTS, HID), F32),
            pltpu.VMEM((SLOTS, HID), BF),
            pltpu.VMEM((SLOTS, HID), BF),
            pltpu.VMEM((SLOTS, HID), BF),
            pltpu.VMEM((NX, SLOTS, FEAT), BF),
            pltpu.VMEM((NX, SLOTS, FEAT), BF),
            *quarter,
            *full,
            *mid,
            *last,
            pltpu.VMEM((NY, 8, 128), F32),
            pltpu.VMEM((3, 8, 128), F32),
            pltpu.VMEM((8, 128), F32),
            pltpu.VMEM((8, 8, 128), F32),
            pltpu.VMEM((NZ, 8, 256), BF),
            pltpu.VMEM((NZ, 8, 256), BF),
            pltpu.SemaphoreType.DMA((130,)),
            pltpu.SemaphoreType.DMA((130,)),
        ],
        compiler_params=pltpu.CompilerParams(
            collective_id=0, has_side_effects=True, vmem_limit_bytes=60 << 20
        ),
    )(*arguments)


def emit_kernel(*refs):
    sources, targets, stage, load_sem, store_sem = refs[:5], refs[5:10], refs[10:15], refs[15], refs[16]
    pieces = [(i, None) for i in range(2)]
    pieces += [(i, part) for part in range(2) for i in range(2, 5)]

    def view(ref, part):
        if part is None:
            return ref
        half = ref.shape[1] // 2
        return ref.at[:, pl.ds(part * half, half)]

    loads = [
        pltpu.make_async_copy(view(sources[i], part), view(stage[i], part), load_sem.at[n])
        for n, (i, part) in enumerate(pieces)
    ]
    stores = [
        pltpu.make_async_copy(view(stage[i], part), view(targets[i], part), store_sem.at[n])
        for n, (i, part) in enumerate(pieces)
    ]
    for copy in loads:
        copy.start()
    for load, store in zip(loads, stores):
        load.wait()
        store.start()
    for copy in stores:
        copy.wait()


def emit(*results):
    return pl.pallas_call(
        emit_kernel,
        name="emit",
        out_shape=tuple(jax.ShapeDtypeStruct(one.shape, one.dtype) for one in results),
        in_specs=[HBM] * 5,
        out_specs=(HBM,) * 5,
        scratch_shapes=[
            *[pltpu.VMEM(one.shape, one.dtype) for one in results],
            pltpu.SemaphoreType.DMA((8,)),
            pltpu.SemaphoreType.DMA((8,)),
        ],
        compiler_params=pltpu.CompilerParams(vmem_limit_bytes=60 << 20),
    )(*results)


def shards(tokens, cotangent, gates, experts, w_gate, w_up, w_down):
    results = layer(tokens, cotangent, gates.T, experts.T, w_gate, w_up, w_down)
    input_grad, routing_grad, gate_grad, up_grad, down_grad = emit(*results)
    return input_grad, routing_grad.T, gate_grad, up_grad, down_grad


def solution(mesh):
    return jax.shard_map(
        shards,
        mesh=mesh,
        in_specs=(
            P("wide", "tensor"),
            P("wide", "tensor"),
            P("wide", None),
            P("wide", None),
            P("wide", None, "tensor"),
            P("wide", None, "tensor"),
            P("wide", "tensor", None),
        ),
        out_specs=(
            P("wide", "tensor"),
            P("wide", None),
            P("wide", None, "tensor"),
            P("wide", None, "tensor"),
            P("wide", "tensor", None),
        ),
        check_vma=False,
    )
```

```python
import jax
import jax.numpy as jnp
from jax import lax
from jax.experimental import pallas as pl
from jax.experimental.pallas import tpu as pltpu
from jax.sharding import PartitionSpec as P

MESH = pl.DeviceIdType.MESH
NZ, NY, NX = 16, 4, 4
TOK = 8
D = 3072
FEAT = 384
HID = 128
ROWS = 64
SLOTS = 256
BF = jnp.bfloat16
F32 = jnp.float32
VMEM = pl.BlockSpec(memory_space=pltpu.VMEM)
HBM = pl.BlockSpec(memory_space=pltpu.MemorySpace.HBM)
Z_ORDER = (8, 7, 9, 6, 10, 5, 11, 4, 12, 3, 13, 2, 14, 1, 15)


def position():
    tensor, wide = lax.axis_index("tensor"), lax.axis_index("wide")
    return (
        lax.div(tensor, 2),
        lax.rem(tensor, 2),
        lax.div(wide, NY),
        lax.rem(wide, NY),
    )


def device_of(x, core, z, y):
    return {"tensor": x * 2 + core, "wide": z * NY + y}


def wrap(value, size):
    return lax.rem(value + size, size)


def dot(left, right, left_dim, right_dim):
    return lax.dot_general(
        left, right, (((left_dim,), (right_dim,)), ((), ())), preferred_element_type=F32
    )


class Wire:
    def __init__(self, send_sem, recv_sem):
        self.send_sem, self.recv_sem = send_sem, recv_sem
        self.sent = []

    def make(self, number, source, target, device):
        return pltpu.make_async_remote_copy(
            src_ref=source,
            dst_ref=target,
            send_sem=self.send_sem.at[number],
            recv_sem=self.recv_sem.at[number],
            device_id=device,
            device_id_type=MESH,
        )

    def send(self, number, source, target, device):
        copy = self.make(number, source, target, device)
        copy.start()
        self.sent.append(copy)

    def arrived(self, number, landed, device):
        self.make(number, landed, landed, device).wait_recv()

    def drain(self):
        for copy in self.sent:
            copy.wait_send()
        self.sent = []


def slot_match(experts, rows, per_expert):
    row = lax.broadcasted_iota(jnp.int32, (rows, TOK), 0)
    expert, half, slot = row // per_expert, (row // 4) % 2, row % 4
    one, zero = jnp.ones((rows, TOK), F32), jnp.zeros((rows, TOK), F32)
    first = jnp.where(jnp.broadcast_to(experts[0:1], (rows, TOK)) == expert, one, zero)
    second = jnp.where(jnp.broadcast_to(experts[1:2], (rows, TOK)) == expert, one, zero)
    left = lax.broadcasted_iota(jnp.int32, (TOK, TOK), 0)
    right = lax.broadcasted_iota(jnp.int32, (TOK, TOK), 1)
    earlier = jnp.where(left < right, 1.0, 0.0).astype(F32)
    before = dot(first + second, earlier, 1, 0)
    at_slot = jnp.where(before == slot.astype(F32), one, zero)
    upper = jnp.where(half == 0, one, zero)
    return first * at_slot, second * at_slot, upper


def selection(wanted):
    column = lax.broadcasted_iota(jnp.int32, (128, 128), 1)
    return jnp.where(column == wanted, 1.0, 0.0).astype(BF)


class Gather:
    def __init__(self, wire, ref, base, place, swap, first_peers, second_peers, sibling):
        self.wire, self.ref, self.base, self.swap, self.sibling = wire, ref, base, swap, sibling
        self.x, self.core, self.y = place
        self.first_peers, self.second_peers = first_peers, second_peers

    def at(self, a, b, ci):
        dx, dy = (b, a) if self.swap else (a, b)
        xi, yi = wrap(self.x - dx, NX), wrap(self.y - dy, NY)
        return self.ref.at[
            pl.ds(pl.multiple_of(yi * ROWS, ROWS), ROWS),
            pl.ds(pl.multiple_of((xi * 2 + ci) * FEAT, 128), FEAT),
        ]

    def push(self, number, piece, device):
        self.wire.send(self.base + number, piece, piece, device)

    def got(self, number, piece):
        self.wire.arrived(self.base + number, piece, self.sibling)

    def start(self):
        for d in (2, 1, 3):
            self.push(d - 1, self.at(0, 0, self.core), self.first_peers[d - 1])

    def spread(self, k):
        block = self.at(k, 0, self.core)
        if k:
            self.got(k - 1, block)
        for d in (2, 1, 3):
            self.push(3 * k + 2 + d, block, self.second_peers[d - 1])

    def feed(self, k, m):
        block = self.at(k, m, self.core)
        if m:
            self.got(3 * k + 2 + m, block)
        self.push(15 + 4 * k + m, block, self.sibling)

    def from_sibling(self):
        for k in range(4):
            for m in range(4):
                self.got(15 + 4 * k + m, self.at(k, m, 1 - self.core))


class Scatter:
    def __init__(self, wire, base, buffers, a, b, first_peers, second_peers):
        self.wire, self.base = wire, base
        self.acc, self.full, self.mid, self.last = buffers
        self.a, self.b = a, b
        self.first_peers, self.second_peers = first_peers, second_peers

    def send(self, d):
        self.wire.send(
            self.base + d - 1,
            self.acc.at[wrap(self.a + d, 4)],
            self.full.at[d - 1],
            self.first_peers[d - 1],
        )

    def send_piece(self, k, i):
        for d in (2, 1, 3):
            self.wire.send(
                self.base + 6 + 3 * k + d - 1,
                self.acc.at[wrap(self.a + d, 4), i],
                self.full.at[d - 1, i],
                self.first_peers[d - 1],
            )

    def pieces(self, order):
        for k, i in enumerate(order):
            for d in (1, 3, 2):
                self.wire.arrived(
                    self.base + 6 + 3 * k + d - 1, self.full.at[d - 1, i], self.first_peers[0]
                )

    def chunks(self):
        for d in (1, 3, 2):
            self.wire.arrived(self.base + d - 1, self.full.at[d - 1], self.first_peers[0])

    def across(self):
        for d in (2, 1, 3, 0):
            i = wrap(self.b + d, 4)
            total = self.acc[self.a, i].astype(F32)
            for e in range(3):
                total = total + self.full[e, i].astype(F32)
            self.mid[i] = total.astype(BF)
            if d:
                self.wire.send(
                    self.base + 2 + d,
                    self.mid.at[i],
                    self.last.at[d - 1],
                    self.second_peers[d - 1],
                )

    def total(self):
        result = self.mid[self.b].astype(F32)
        for d in range(1, 4):
            self.wire.arrived(self.base + 2 + d, self.last.at[d - 1], self.second_peers[0])
            result = result + self.last[d - 1].astype(F32)
        return result


def layer_kernel(
    tokens_hbm,
    cotangent_hbm,
    gates_hbm,
    experts_hbm,
    wg_hbm,
    wu_hbm,
    wd_hbm,
    grad_hbm,
    routing_hbm,
    dwg_hbm,
    dwu_hbm,
    dwd_hbm,
    grad_ref,
    routing_ref,
    tokens_ref,
    cotangent_ref,
    gates_ref,
    experts_ref,
    wg_ref,
    wu_ref,
    wd_ref,
    dwg_ref,
    dwu_ref,
    dwd_ref,
    load_sem,
    out_buf,
    in_buf,
    x_ref,
    c_ref,
    sums,
    gg_ref,
    gu_ref,
    hid_ref,
    r_out,
    r_in,
    acc_p,
    acc_q,
    full_p,
    full_q,
    mid_p,
    mid_q,
    last_p,
    last_q,
    t_ref,
    t_y,
    t_sum,
    t_t,
    back_out,
    back_in,
    send_sem,
    recv_sem,
):
    x, core, z, y = position()
    tensor = x * 2 + core
    small = [
        pltpu.make_async_copy(source, target, load_sem.at[i])
        for i, (source, target) in enumerate(
            (
                (experts_hbm, experts_ref),
                (gates_hbm, gates_ref),
                (tokens_hbm, tokens_ref),
                (cotangent_hbm, cotangent_ref),
            )
        )
    ]
    weights = [
        pltpu.make_async_copy(source, target, load_sem.at[4 + i])
        for i, (source, target) in enumerate(
            ((wg_hbm, wg_ref), (wu_hbm, wu_ref), (wd_hbm, wd_ref))
        )
    ]
    for copy in small:
        copy.start()
    peers_z = [device_of(x, core, wrap(z + d, NZ), y) for d in range(1, NZ)]
    peers_t = [{"tensor": wrap(tensor + d, 8), "wide": z * NY + y} for d in range(1, 8)]
    peers_y = [device_of(x, core, z, wrap(y + d, NY)) for d in range(1, NY)]
    peers_x = [device_of(wrap(x + d, NX), core, z, y) for d in range(1, NX)]
    sibling = device_of(x, 1 - core, z, y)

    barrier = pltpu.get_barrier_semaphore()
    partners = [peers_z[d - 1] for d in Z_ORDER] + peers_y + peers_t
    for partner in partners:
        pl.semaphore_signal(barrier, inc=1, device_id=partner, device_id_type=MESH)
    for copy in weights:
        copy.start()
    for copy in small:
        copy.wait()

    first, second, upper = slot_match(experts_ref[...], 64, 8)
    gates = gates_ref[...].astype(F32)
    pick_in = ((first + second) * upper).astype(BF)
    pick_up = ((first * gates[0:1] + second * gates[1:2]) * (1.0 - upper)).astype(BF)
    chosen = dot(pick_in, tokens_ref[...], 1, 0) + dot(pick_up, cotangent_ref[...], 1, 0)
    out_buf[...] = chosen.reshape(8, 8, FEAT).astype(BF)
    pl.semaphore_wait(barrier, len(partners))

    wire = Wire(send_sem, recv_sem)
    for d in Z_ORDER:
        there = wrap(z + d, NZ)
        wire.send(d - 1, out_buf.at[lax.div(there, 2)], in_buf.at[z], peers_z[d - 1])
    in_buf[z] = out_buf[lax.div(z, 2)]
    for d in Z_ORDER[::-1]:
        wire.arrived(d - 1, in_buf.at[wrap(z - d, NZ)], sibling)

    out_row = lax.broadcasted_iota(jnp.int32, (128, 128), 0)
    order = selection((out_row % 64) // 4 * 8 + out_row // 64 * 4 + out_row % 4)
    came = in_buf[...].astype(F32).reshape(128, FEAT).astype(BF)
    arranged = dot(order, came, 1, 0).astype(BF)
    my_rows = pl.ds(pl.multiple_of(y * ROWS, ROWS), ROWS)
    my_columns = pl.ds(pl.multiple_of(tensor * FEAT, 128), FEAT)
    x_ref[my_rows, my_columns] = arranged[0:64]
    c_ref[my_rows, my_columns] = arranged[64:128]

    place = (x, core, y)
    gathers = (
        Gather(wire, x_ref, 15, place, False, peers_x, peers_y, sibling),
        Gather(wire, c_ref, 46, place, True, peers_y, peers_x, sibling),
    )
    for one in gathers:
        one.start()
    for one in gathers:
        one.spread(0)
    for k in (1, 3, 2):
        for one in gathers:
            one.spread(k)
    for k in (0, 1, 3, 2):
        for m in (0, 1, 3, 2):
            for one in gathers:
                one.feed(k, m)

    def columns_of(xi, ci):
        return pl.ds(pl.multiple_of((xi * 2 + ci) * FEAT, 128), FEAT)

    def forward(ci):
        gate = up = through = None
        for xi in range(NX):
            columns = columns_of(xi, ci)
            terms = (
                dot(x_ref[:, columns], wg_ref[0, columns, :], 1, 0),
                dot(x_ref[:, columns], wu_ref[0, columns, :], 1, 0),
                dot(c_ref[:, columns], wd_ref[0, :, columns], 1, 1),
            )
            if gate is None:
                gate, up, through = terms
            else:
                gate, up, through = gate + terms[0], up + terms[1], through + terms[2]
        return gate, up, through

    for copy in weights:
        copy.wait()
    sums[0], sums[1], sums[2] = forward(core)
    for one in gathers:
        one.from_sibling()
    pre_gate, pre_up, hidden_grad = forward(1 - core)
    pre_gate, pre_up, hidden_grad = pre_gate + sums[0], pre_up + sums[1], hidden_grad + sums[2]
    sig = jax.nn.sigmoid(pre_gate)
    act = pre_gate * sig
    hidden = act * pre_up
    gg_ref[...] = (hidden_grad * pre_up * sig * (1.0 + pre_gate * (1.0 - sig))).astype(BF)
    gu_ref[...] = (hidden_grad * act).astype(BF)

    def returned(xi, ci):
        columns = columns_of(xi, ci)
        return dot(gg_ref[...], wg_ref[0, columns, :], 1, 1) + dot(
            gu_ref[...], wu_ref[0, columns, :], 1, 1
        )

    scatters = (
        Scatter(wire, 94, (acc_p, full_p, mid_p, last_p), x, y, peers_x, peers_y),
        Scatter(wire, 130, (acc_q, full_q, mid_q, last_q), y, x, peers_y, peers_x),
    )
    x_order = (2, 1, 3, 0)
    for k, d in enumerate(x_order):
        r_out[k] = returned(wrap(x + d, NX), 1 - core).astype(BF)
        wire.send(90 + k, r_out.at[k], r_in.at[k], sibling)
    hid_ref[...] = hidden.astype(BF)
    row = lax.broadcasted_iota(jnp.int32, (ROWS, 128), 0)
    lane = lax.broadcasted_iota(jnp.int32, (ROWS, 128), 1)
    row_sums = jnp.sum(hidden_grad * hidden, axis=1, keepdims=True)
    for yi in range(NY):
        part = jnp.broadcast_to(row_sums[yi * ROWS : (yi + 1) * ROWS], (ROWS, 128))
        line = jnp.sum(jnp.where(row == lane, part, 0.0), axis=0, keepdims=True)
        t_ref[yi] = jnp.broadcast_to(line, (8, 128))
    for d in range(1, NY):
        wire.send(86 + d, t_ref.at[wrap(y + d, NY)], t_y.at[d - 1], peers_y[d - 1])
    for k, d in enumerate(x_order):
        xi = wrap(x + d, NX)
        own = returned(xi, core)
        wire.arrived(90 + k, r_in.at[k], sibling)
        total = (own + r_in[k].astype(F32)).astype(BF)
        for yi in range(NY):
            acc_p[xi, yi] = total[yi * ROWS : yi * ROWS + 32]
            acc_q[yi, xi] = total[yi * ROWS + 32 : yi * ROWS + 64]
        if d:
            scatters[0].send(d)
        scatters[1].send_piece(k, xi)

    def weight_grads(which):
        step = 512
        for k in range(D // step):
            rows = pl.ds(k * step, step)
            if which == 0:
                dwd_ref[0, :, rows] = dot(hid_ref[...], c_ref[:, rows], 0, 0).astype(BF)
            if which == 1:
                dwg_ref[0, rows, :] = dot(x_ref[:, rows], gg_ref[...], 0, 0).astype(BF)
            if which == 2:
                dwu_ref[0, rows, :] = dot(x_ref[:, rows], gu_ref[...], 0, 0).astype(BF)

    stores = [
        pltpu.make_async_copy(source, target, load_sem.at[7 + i])
        for i, (source, target) in enumerate(
            ((dwd_ref, dwd_hbm), (dwg_ref, dwg_hbm), (dwu_ref, dwu_hbm))
        )
    ]
    line = t_ref[y]
    for d in range(1, NY):
        wire.arrived(86 + d, t_y.at[d - 1], sibling)
        line = line + t_y[d - 1]
    t_sum[...] = line
    t_t[tensor] = line
    for d in range(1, 8):
        wire.send(107 + d, t_sum, t_t.at[tensor], peers_t[d - 1])
    weight_grads(0)
    stores[0].start()
    weight_grads(1)
    stores[1].start()
    scatters[1].pieces([wrap(x + d, NX) for d in x_order])
    scatters[1].across()
    scatters[0].chunks()
    scatters[0].across()
    weight_grads(2)
    stores[2].start()
    for d in range(1, 8):
        wire.arrived(107 + d, t_t.at[wrap(tensor - d, 8)], sibling)
    line = t_t[0]
    for i in range(1, 8):
        line = line + t_t[i]
    spread = jnp.where(row == lane, jnp.broadcast_to(line[0:1], (ROWS, 128)), 0.0)
    column = jnp.broadcast_to(jnp.sum(spread, axis=1, keepdims=True), (ROWS, 128))
    result = jnp.concatenate([one.total() for one in scatters], axis=0)
    pair = jnp.concatenate(
        [
            result[:, 0:256],
            jnp.concatenate([result[:, 256:FEAT], column], axis=1),
        ],
        axis=0,
    ).astype(BF)
    order = selection((out_row // 4) % 2 * 64 + out_row // 8 * 4 + out_row % 4)
    back_out[...] = dot(order, pair, 1, 0).reshape(NZ, 8, 256).astype(BF)
    earlier = Wire(send_sem, recv_sem)
    earlier.sent, wire.sent = wire.sent, []
    for d in Z_ORDER:
        wire.send(114 + d, back_out.at[wrap(z + d, NZ)], back_in.at[z], peers_z[d - 1])
    back_in[z] = back_out[z]

    first, second, upper = slot_match(experts_ref[...], 128, 16)
    lower = 1.0 - upper
    pick_head = ((first + second) * upper).astype(BF)
    pick_tail = ((first + second) * lower).astype(BF)
    pick_first = (first * lower).astype(BF)
    pick_second = (second * lower).astype(BF)
    earlier.drain()
    for copy in stores:
        copy.wait()
    for d in Z_ORDER[::-1]:
        wire.arrived(114 + d, back_in.at[wrap(z - d, NZ)], sibling)
    came = back_in[...].astype(F32).reshape(128, 256).astype(BF)
    grad_ref[:, 0:256] = dot(pick_head, came, 0, 0).astype(BF)
    grad_ref[:, 256:FEAT] = dot(pick_tail, came[:, 0:128], 0, 0).astype(BF)
    results = [
        pltpu.make_async_copy(grad_ref, grad_hbm, load_sem.at[0]),
        pltpu.make_async_copy(routing_ref, routing_hbm, load_sem.at[1]),
    ]
    results[0].start()
    at_first = dot(came[:, 128:], pick_first, 0, 0)
    at_second = dot(came[:, 128:], pick_second, 0, 0)
    routing_ref[0:1, :] = at_first[0:1, :] / gates[0:1]
    routing_ref[1:2, :] = at_second[0:1, :] / gates[1:2]
    results[1].start()
    wire.drain()
    for copy in results:
        copy.wait()


def layer(*arguments):
    quarter = [pltpu.VMEM((4, 4, 32, FEAT), BF)] * 2
    full = [pltpu.VMEM((3, 4, 32, FEAT), BF)] * 2
    mid = [pltpu.VMEM((4, 32, FEAT), BF)] * 2
    last = [pltpu.VMEM((3, 32, FEAT), BF)] * 2
    return pl.pallas_call(
        layer_kernel,
        name="layer",
        out_shape=(
            jax.ShapeDtypeStruct((TOK, FEAT), BF),
            jax.ShapeDtypeStruct((2, TOK), F32),
            jax.ShapeDtypeStruct((1, D, HID), BF),
            jax.ShapeDtypeStruct((1, D, HID), BF),
            jax.ShapeDtypeStruct((1, HID, D), BF),
        ),
        in_specs=[HBM] * 7,
        out_specs=(HBM,) * 5,
        scratch_shapes=[
            pltpu.VMEM((TOK, FEAT), BF),
            pltpu.VMEM((2, TOK), F32),
            pltpu.VMEM((TOK, FEAT), BF),
            pltpu.VMEM((TOK, FEAT), BF),
            pltpu.VMEM((2, TOK), BF),
            pltpu.VMEM((2, TOK), jnp.int32),
            pltpu.VMEM((1, D, HID), BF),
            pltpu.VMEM((1, D, HID), BF),
            pltpu.VMEM((1, HID, D), BF),
            pltpu.VMEM((1, D, HID), BF),
            pltpu.VMEM((1, D, HID), BF),
            pltpu.VMEM((1, HID, D), BF),
            pltpu.SemaphoreType.DMA((10,)),
            pltpu.VMEM((8, 8, FEAT), BF),
            pltpu.VMEM((NZ, 8, FEAT), BF),
            pltpu.VMEM((SLOTS, D), BF),
            pltpu.VMEM((SLOTS, D), BF),
            pltpu.VMEM((3, SLOTS, HID), F32),
            pltpu.VMEM((SLOTS, HID), BF),
            pltpu.VMEM((SLOTS, HID), BF),
            pltpu.VMEM((SLOTS, HID), BF),
            pltpu.VMEM((NX, SLOTS, FEAT), BF),
            pltpu.VMEM((NX, SLOTS, FEAT), BF),
            *quarter,
            *full,
            *mid,
            *last,
            pltpu.VMEM((NY, 8, 128), F32),
            pltpu.VMEM((3, 8, 128), F32),
            pltpu.VMEM((8, 128), F32),
            pltpu.VMEM((8, 8, 128), F32),
            pltpu.VMEM((NZ, 8, 256), BF),
            pltpu.VMEM((NZ, 8, 256), BF),
            pltpu.SemaphoreType.DMA((148,)),
            pltpu.SemaphoreType.DMA((148,)),
        ],
        compiler_params=pltpu.CompilerParams(
            collective_id=0, has_side_effects=True, vmem_limit_bytes=60 << 20
        ),
    )(*arguments)


def emit_kernel(*refs):
    sources, targets, stage, load_sem, store_sem = refs[:5], refs[5:10], refs[10:15], refs[15], refs[16]
    pieces = [(i, None) for i in range(2)]
    pieces += [(i, part) for part in range(2) for i in range(2, 5)]

    def view(ref, part):
        if part is None:
            return ref
        half = ref.shape[1] // 2
        return ref.at[:, pl.ds(part * half, half)]

    loads = [
        pltpu.make_async_copy(view(sources[i], part), view(stage[i], part), load_sem.at[n])
        for n, (i, part) in enumerate(pieces)
    ]
    stores = [
        pltpu.make_async_copy(view(stage[i], part), view(targets[i], part), store_sem.at[n])
        for n, (i, part) in enumerate(pieces)
    ]
    for copy in loads:
        copy.start()
    for load, store in zip(loads, stores):
        load.wait()
        store.start()
    for copy in stores:
        copy.wait()


def emit(*results):
    return pl.pallas_call(
        emit_kernel,
        name="emit",
        out_shape=tuple(jax.ShapeDtypeStruct(one.shape, one.dtype) for one in results),
        in_specs=[HBM] * 5,
        out_specs=(HBM,) * 5,
        scratch_shapes=[
            *[pltpu.VMEM(one.shape, one.dtype) for one in results],
            pltpu.SemaphoreType.DMA((8,)),
            pltpu.SemaphoreType.DMA((8,)),
        ],
        compiler_params=pltpu.CompilerParams(vmem_limit_bytes=60 << 20),
    )(*results)


def shards(tokens, cotangent, gates, experts, w_gate, w_up, w_down):
    results = layer(tokens, cotangent, gates.T, experts.T, w_gate, w_up, w_down)
    input_grad, routing_grad, gate_grad, up_grad, down_grad = emit(*results)
    return input_grad, routing_grad.T, gate_grad, up_grad, down_grad


def solution(mesh):
    return jax.shard_map(
        shards,
        mesh=mesh,
        in_specs=(
            P("wide", "tensor"),
            P("wide", "tensor"),
            P("wide", None),
            P("wide", None),
            P("wide", None, "tensor"),
            P("wide", None, "tensor"),
            P("wide", "tensor", None),
        ),
        out_specs=(
            P("wide", "tensor"),
            P("wide", None),
            P("wide", None, "tensor"),
            P("wide", None, "tensor"),
            P("wide", "tensor", None),
        ),
        check_vma=False,
    )
```

```python
import jax
import jax.numpy as jnp
from jax import lax
from jax.experimental import pallas as pl
from jax.experimental.pallas import tpu as pltpu
from jax.sharding import PartitionSpec as P

MESH = pl.DeviceIdType.MESH
NZ, NY, NX = 16, 4, 4
TOK = 8
D = 3072
FEAT = 384
HID = 128
ROWS = 64
SLOTS = 256
BF = jnp.bfloat16
F32 = jnp.float32
VMEM = pl.BlockSpec(memory_space=pltpu.VMEM)
HBM = pl.BlockSpec(memory_space=pltpu.MemorySpace.HBM)
Z_ORDER = (8, 7, 9, 6, 10, 5, 11, 4, 12, 3, 13, 2, 14, 1, 15)


def position():
    tensor, wide = lax.axis_index("tensor"), lax.axis_index("wide")
    return (
        lax.div(tensor, 2),
        lax.rem(tensor, 2),
        lax.div(wide, NY),
        lax.rem(wide, NY),
    )


def device_of(x, core, z, y):
    return {"tensor": x * 2 + core, "wide": z * NY + y}


def wrap(value, size):
    return lax.rem(value + size, size)


def dot(left, right, left_dim, right_dim):
    return lax.dot_general(
        left, right, (((left_dim,), (right_dim,)), ((), ())), preferred_element_type=F32
    )


class Wire:
    def __init__(self, send_sem, recv_sem):
        self.send_sem, self.recv_sem = send_sem, recv_sem
        self.sent = []

    def make(self, number, source, target, device):
        return pltpu.make_async_remote_copy(
            src_ref=source,
            dst_ref=target,
            send_sem=self.send_sem.at[number],
            recv_sem=self.recv_sem.at[number],
            device_id=device,
            device_id_type=MESH,
        )

    def send(self, number, source, target, device):
        copy = self.make(number, source, target, device)
        copy.start()
        self.sent.append(copy)

    def arrived(self, number, landed, device):
        self.make(number, landed, landed, device).wait_recv()

    def drain(self):
        for copy in self.sent:
            copy.wait_send()
        self.sent = []


def slot_match(experts, rows, per_expert):
    row = lax.broadcasted_iota(jnp.int32, (rows, TOK), 0)
    expert, half, slot = row // per_expert, (row // 4) % 2, row % 4
    one, zero = jnp.ones((rows, TOK), F32), jnp.zeros((rows, TOK), F32)
    first = jnp.where(jnp.broadcast_to(experts[0:1], (rows, TOK)) == expert, one, zero)
    second = jnp.where(jnp.broadcast_to(experts[1:2], (rows, TOK)) == expert, one, zero)
    left = lax.broadcasted_iota(jnp.int32, (TOK, TOK), 0)
    right = lax.broadcasted_iota(jnp.int32, (TOK, TOK), 1)
    earlier = jnp.where(left < right, 1.0, 0.0).astype(F32)
    before = dot(first + second, earlier, 1, 0)
    at_slot = jnp.where(before == slot.astype(F32), one, zero)
    upper = jnp.where(half == 0, one, zero)
    return first * at_slot, second * at_slot, upper


def selection(wanted):
    column = lax.broadcasted_iota(jnp.int32, (128, 128), 1)
    return jnp.where(column == wanted, 1.0, 0.0).astype(BF)


class Gather:
    def __init__(self, wire, ref, base, place, swap, first_peers, second_peers, sibling):
        self.wire, self.ref, self.base, self.swap, self.sibling = wire, ref, base, swap, sibling
        self.x, self.core, self.y = place
        self.first_peers, self.second_peers = first_peers, second_peers

    def at(self, a, b, ci):
        dx, dy = (b, a) if self.swap else (a, b)
        xi, yi = wrap(self.x - dx, NX), wrap(self.y - dy, NY)
        return self.ref.at[
            pl.ds(pl.multiple_of(yi * ROWS, ROWS), ROWS),
            pl.ds(pl.multiple_of((xi * 2 + ci) * FEAT, 128), FEAT),
        ]

    def push(self, number, piece, device):
        self.wire.send(self.base + number, piece, piece, device)

    def got(self, number, piece):
        self.wire.arrived(self.base + number, piece, self.sibling)

    def start(self):
        for d in (2, 1, 3):
            self.push(d - 1, self.at(0, 0, self.core), self.first_peers[d - 1])

    def spread(self, k):
        block = self.at(k, 0, self.core)
        if k:
            self.got(k - 1, block)
        for d in (2, 1, 3):
            self.push(3 * k + 2 + d, block, self.second_peers[d - 1])

    def feed(self, k, m):
        block = self.at(k, m, self.core)
        if m:
            self.got(3 * k + 2 + m, block)
        self.push(15 + 4 * k + m, block, self.sibling)

    def from_sibling(self):
        for k in range(4):
            for m in range(4):
                self.got(15 + 4 * k + m, self.at(k, m, 1 - self.core))


class Scatter:
    def __init__(self, wire, base, buffers, a, b, first_peers, second_peers):
        self.wire, self.base = wire, base
        self.acc, self.full, self.mid, self.last = buffers
        self.a, self.b = a, b
        self.first_peers, self.second_peers = first_peers, second_peers

    def send(self, d):
        self.wire.send(
            self.base + d - 1,
            self.acc.at[wrap(self.a + d, 4)],
            self.full.at[d - 1],
            self.first_peers[d - 1],
        )

    def send_piece(self, k, i):
        for d in (2, 1, 3):
            self.wire.send(
                self.base + 6 + 3 * k + d - 1,
                self.acc.at[wrap(self.a + d, 4), i],
                self.full.at[d - 1, i],
                self.first_peers[d - 1],
            )

    def pieces(self, order):
        for k, i in enumerate(order):
            for d in (1, 3, 2):
                self.wire.arrived(
                    self.base + 6 + 3 * k + d - 1, self.full.at[d - 1, i], self.first_peers[0]
                )

    def chunks(self):
        for d in (1, 3, 2):
            self.wire.arrived(self.base + d - 1, self.full.at[d - 1], self.first_peers[0])

    def across(self):
        for d in (2, 1, 3, 0):
            i = wrap(self.b + d, 4)
            total = self.acc[self.a, i].astype(F32)
            for e in range(3):
                total = total + self.full[e, i].astype(F32)
            self.mid[i] = total.astype(BF)
            if d:
                self.wire.send(
                    self.base + 2 + d,
                    self.mid.at[i],
                    self.last.at[d - 1],
                    self.second_peers[d - 1],
                )

    def total(self):
        result = self.mid[self.b].astype(F32)
        for d in range(1, 4):
            self.wire.arrived(self.base + 2 + d, self.last.at[d - 1], self.second_peers[0])
            result = result + self.last[d - 1].astype(F32)
        return result


def layer_kernel(
    tokens_hbm,
    cotangent_hbm,
    gates_hbm,
    experts_hbm,
    wg_hbm,
    wu_hbm,
    wd_hbm,
    grad_hbm,
    routing_hbm,
    dwg_hbm,
    dwu_hbm,
    dwd_hbm,
    grad_ref,
    routing_ref,
    tokens_ref,
    cotangent_ref,
    gates_ref,
    experts_ref,
    wg_ref,
    wu_ref,
    wd_ref,
    dwg_ref,
    dwu_ref,
    dwd_ref,
    load_sem,
    out_buf,
    in_buf,
    x_ref,
    c_ref,
    sums,
    gg_ref,
    gu_ref,
    hid_ref,
    r_out,
    r_in,
    acc_p,
    acc_q,
    full_p,
    full_q,
    mid_p,
    mid_q,
    last_p,
    last_q,
    t_ref,
    t_y,
    t_sum,
    t_t,
    back_out,
    back_in,
    send_sem,
    recv_sem,
):
    x, core, z, y = position()
    tensor = x * 2 + core
    small = [
        pltpu.make_async_copy(source, target, load_sem.at[i])
        for i, (source, target) in enumerate(
            (
                (experts_hbm, experts_ref),
                (gates_hbm, gates_ref),
                (tokens_hbm, tokens_ref),
                (cotangent_hbm, cotangent_ref),
            )
        )
    ]
    weights = [
        pltpu.make_async_copy(source, target, load_sem.at[4 + i])
        for i, (source, target) in enumerate(
            ((wg_hbm, wg_ref), (wu_hbm, wu_ref), (wd_hbm, wd_ref))
        )
    ]
    for copy in small:
        copy.start()
    peers_z = [device_of(x, core, wrap(z + d, NZ), y) for d in range(1, NZ)]
    peers_t = [{"tensor": wrap(tensor + d, 8), "wide": z * NY + y} for d in range(1, 8)]
    peers_y = [device_of(x, core, z, wrap(y + d, NY)) for d in range(1, NY)]
    peers_x = [device_of(wrap(x + d, NX), core, z, y) for d in range(1, NX)]
    sibling = device_of(x, 1 - core, z, y)

    barrier = pltpu.get_barrier_semaphore()
    partners = [peers_z[d - 1] for d in Z_ORDER] + peers_y + peers_t
    for partner in partners:
        pl.semaphore_signal(barrier, inc=1, device_id=partner, device_id_type=MESH)
    for copy in weights:
        copy.start()
    for copy in small:
        copy.wait()

    first, second, upper = slot_match(experts_ref[...], 64, 8)
    gates = gates_ref[...].astype(F32)
    pick_in = ((first + second) * upper).astype(BF)
    pick_up = ((first * gates[0:1] + second * gates[1:2]) * (1.0 - upper)).astype(BF)
    chosen = dot(pick_in, tokens_ref[...], 1, 0) + dot(pick_up, cotangent_ref[...], 1, 0)
    out_buf[...] = chosen.reshape(8, 8, FEAT).astype(BF)
    pl.semaphore_wait(barrier, len(partners))

    wire = Wire(send_sem, recv_sem)
    for d in Z_ORDER:
        there = wrap(z + d, NZ)
        wire.send(d - 1, out_buf.at[lax.div(there, 2)], in_buf.at[z], peers_z[d - 1])
    in_buf[z] = out_buf[lax.div(z, 2)]
    for d in Z_ORDER[::-1]:
        wire.arrived(d - 1, in_buf.at[wrap(z - d, NZ)], sibling)

    out_row = lax.broadcasted_iota(jnp.int32, (128, 128), 0)
    order = selection((out_row % 64) // 4 * 8 + out_row // 64 * 4 + out_row % 4)
    came = in_buf[...].astype(F32).reshape(128, FEAT).astype(BF)
    arranged = dot(order, came, 1, 0).astype(BF)
    my_rows = pl.ds(pl.multiple_of(y * ROWS, ROWS), ROWS)
    my_columns = pl.ds(pl.multiple_of(tensor * FEAT, 128), FEAT)
    x_ref[my_rows, my_columns] = arranged[0:64]
    c_ref[my_rows, my_columns] = arranged[64:128]

    place = (x, core, y)
    gathers = (
        Gather(wire, x_ref, 15, place, False, peers_x, peers_y, sibling),
        Gather(wire, c_ref, 46, place, True, peers_y, peers_x, sibling),
    )
    for one in gathers:
        one.start()
    for one in gathers:
        one.spread(0)
    for k in (1, 3, 2):
        for one in gathers:
            one.spread(k)
    for k in (0, 1, 3, 2):
        for m in (0, 1, 3, 2):
            for one in gathers:
                one.feed(k, m)

    def columns_of(xi, ci):
        return pl.ds(pl.multiple_of((xi * 2 + ci) * FEAT, 128), FEAT)

    def project(ci, upstream):
        parts = None
        for xi in range(NX):
            columns = columns_of(xi, ci)
            if upstream:
                terms = [dot(c_ref[:, columns], wd_ref[0, :, columns], 1, 1)]
            else:
                terms = [
                    dot(x_ref[:, columns], wg_ref[0, columns, :], 1, 0),
                    dot(x_ref[:, columns], wu_ref[0, columns, :], 1, 0),
                ]
            parts = terms if parts is None else [a + b for a, b in zip(parts, terms)]
        return parts

    for copy in weights:
        copy.wait()
    sums[0], sums[1] = project(core, False)
    sums[2] = project(core, True)[0]
    gathers[0].from_sibling()
    pre_gate, pre_up = project(1 - core, False)
    pre_gate, pre_up = pre_gate + sums[0], pre_up + sums[1]
    gathers[1].from_sibling()
    hidden_grad = project(1 - core, True)[0] + sums[2]
    sig = jax.nn.sigmoid(pre_gate)
    act = pre_gate * sig
    hidden = act * pre_up
    gg_ref[...] = (hidden_grad * pre_up * sig * (1.0 + pre_gate * (1.0 - sig))).astype(BF)
    gu_ref[...] = (hidden_grad * act).astype(BF)

    def returned(xi, ci):
        columns = columns_of(xi, ci)
        return dot(gg_ref[...], wg_ref[0, columns, :], 1, 1) + dot(
            gu_ref[...], wu_ref[0, columns, :], 1, 1
        )

    scatters = (
        Scatter(wire, 94, (acc_p, full_p, mid_p, last_p), x, y, peers_x, peers_y),
        Scatter(wire, 130, (acc_q, full_q, mid_q, last_q), y, x, peers_y, peers_x),
    )
    x_order = (2, 1, 3, 0)
    for k, d in enumerate(x_order):
        r_out[k] = returned(wrap(x + d, NX), 1 - core).astype(BF)
        wire.send(90 + k, r_out.at[k], r_in.at[k], sibling)
    hid_ref[...] = hidden.astype(BF)
    row = lax.broadcasted_iota(jnp.int32, (ROWS, 128), 0)
    lane = lax.broadcasted_iota(jnp.int32, (ROWS, 128), 1)
    row_sums = jnp.sum(hidden_grad * hidden, axis=1, keepdims=True)
    for yi in range(NY):
        part = jnp.broadcast_to(row_sums[yi * ROWS : (yi + 1) * ROWS], (ROWS, 128))
        line = jnp.sum(jnp.where(row == lane, part, 0.0), axis=0, keepdims=True)
        t_ref[yi] = jnp.broadcast_to(line, (8, 128))
    for d in range(1, NY):
        wire.send(86 + d, t_ref.at[wrap(y + d, NY)], t_y.at[d - 1], peers_y[d - 1])
    for k, d in enumerate(x_order):
        xi = wrap(x + d, NX)
        own = returned(xi, core)
        wire.arrived(90 + k, r_in.at[k], sibling)
        total = (own + r_in[k].astype(F32)).astype(BF)
        for yi in range(NY):
            acc_p[xi, yi] = total[yi * ROWS : yi * ROWS + 32]
            acc_q[yi, xi] = total[yi * ROWS + 32 : yi * ROWS + 64]
        if d:
            scatters[0].send(d)
        scatters[1].send_piece(k, xi)

    def weight_grads(which):
        step = 512
        for k in range(D // step):
            rows = pl.ds(k * step, step)
            if which == 0:
                dwd_ref[0, :, rows] = dot(hid_ref[...], c_ref[:, rows], 0, 0).astype(BF)
            if which == 1:
                dwg_ref[0, rows, :] = dot(x_ref[:, rows], gg_ref[...], 0, 0).astype(BF)
            if which == 2:
                dwu_ref[0, rows, :] = dot(x_ref[:, rows], gu_ref[...], 0, 0).astype(BF)

    stores = [
        pltpu.make_async_copy(source, target, load_sem.at[7 + i])
        for i, (source, target) in enumerate(
            ((dwd_ref, dwd_hbm), (dwg_ref, dwg_hbm), (dwu_ref, dwu_hbm))
        )
    ]
    line = t_ref[y]
    for d in range(1, NY):
        wire.arrived(86 + d, t_y.at[d - 1], sibling)
        line = line + t_y[d - 1]
    t_sum[...] = line
    t_t[tensor] = line
    for d in range(1, 8):
        wire.send(107 + d, t_sum, t_t.at[tensor], peers_t[d - 1])
    weight_grads(0)
    stores[0].start()
    weight_grads(1)
    stores[1].start()
    scatters[1].pieces([wrap(x + d, NX) for d in x_order])
    scatters[1].across()
    scatters[0].chunks()
    scatters[0].across()
    weight_grads(2)
    stores[2].start()
    for d in range(1, 8):
        wire.arrived(107 + d, t_t.at[wrap(tensor - d, 8)], sibling)
    line = t_t[0]
    for i in range(1, 8):
        line = line + t_t[i]
    spread = jnp.where(row == lane, jnp.broadcast_to(line[0:1], (ROWS, 128)), 0.0)
    column = jnp.broadcast_to(jnp.sum(spread, axis=1, keepdims=True), (ROWS, 128))
    result = jnp.concatenate([one.total() for one in scatters], axis=0)
    pair = jnp.concatenate(
        [
            result[:, 0:256],
            jnp.concatenate([result[:, 256:FEAT], column], axis=1),
        ],
        axis=0,
    ).astype(BF)
    order = selection((out_row // 4) % 2 * 64 + out_row // 8 * 4 + out_row % 4)
    back_out[...] = dot(order, pair, 1, 0).reshape(NZ, 8, 256).astype(BF)
    earlier = Wire(send_sem, recv_sem)
    earlier.sent, wire.sent = wire.sent, []
    for d in Z_ORDER:
        wire.send(114 + d, back_out.at[wrap(z + d, NZ)], back_in.at[z], peers_z[d - 1])
    back_in[z] = back_out[z]

    first, second, upper = slot_match(experts_ref[...], 128, 16)
    lower = 1.0 - upper
    pick_head = ((first + second) * upper).astype(BF)
    pick_tail = ((first + second) * lower).astype(BF)
    pick_first = (first * lower).astype(BF)
    pick_second = (second * lower).astype(BF)
    earlier.drain()
    for copy in stores:
        copy.wait()
    for d in Z_ORDER[::-1]:
        wire.arrived(114 + d, back_in.at[wrap(z - d, NZ)], sibling)
    came = back_in[...].astype(F32).reshape(128, 256).astype(BF)
    grad_ref[:, 0:256] = dot(pick_head, came, 0, 0).astype(BF)
    grad_ref[:, 256:FEAT] = dot(pick_tail, came[:, 0:128], 0, 0).astype(BF)
    results = [
        pltpu.make_async_copy(grad_ref, grad_hbm, load_sem.at[0]),
        pltpu.make_async_copy(routing_ref, routing_hbm, load_sem.at[1]),
    ]
    results[0].start()
    at_first = dot(came[:, 128:], pick_first, 0, 0)
    at_second = dot(came[:, 128:], pick_second, 0, 0)
    routing_ref[0:1, :] = at_first[0:1, :] / gates[0:1]
    routing_ref[1:2, :] = at_second[0:1, :] / gates[1:2]
    results[1].start()
    wire.drain()
    for copy in results:
        copy.wait()


def layer(*arguments):
    quarter = [pltpu.VMEM((4, 4, 32, FEAT), BF)] * 2
    full = [pltpu.VMEM((3, 4, 32, FEAT), BF)] * 2
    mid = [pltpu.VMEM((4, 32, FEAT), BF)] * 2
    last = [pltpu.VMEM((3, 32, FEAT), BF)] * 2
    return pl.pallas_call(
        layer_kernel,
        name="layer",
        out_shape=(
            jax.ShapeDtypeStruct((TOK, FEAT), BF),
            jax.ShapeDtypeStruct((2, TOK), F32),
            jax.ShapeDtypeStruct((1, D, HID), BF),
            jax.ShapeDtypeStruct((1, D, HID), BF),
            jax.ShapeDtypeStruct((1, HID, D), BF),
        ),
        in_specs=[HBM] * 7,
        out_specs=(HBM,) * 5,
        scratch_shapes=[
            pltpu.VMEM((TOK, FEAT), BF),
            pltpu.VMEM((2, TOK), F32),
            pltpu.VMEM((TOK, FEAT), BF),
            pltpu.VMEM((TOK, FEAT), BF),
            pltpu.VMEM((2, TOK), BF),
            pltpu.VMEM((2, TOK), jnp.int32),
            pltpu.VMEM((1, D, HID), BF),
            pltpu.VMEM((1, D, HID), BF),
            pltpu.VMEM((1, HID, D), BF),
            pltpu.VMEM((1, D, HID), BF),
            pltpu.VMEM((1, D, HID), BF),
            pltpu.VMEM((1, HID, D), BF),
            pltpu.SemaphoreType.DMA((10,)),
            pltpu.VMEM((8, 8, FEAT), BF),
            pltpu.VMEM((NZ, 8, FEAT), BF),
            pltpu.VMEM((SLOTS, D), BF),
            pltpu.VMEM((SLOTS, D), BF),
            pltpu.VMEM((3, SLOTS, HID), F32),
            pltpu.VMEM((SLOTS, HID), BF),
            pltpu.VMEM((SLOTS, HID), BF),
            pltpu.VMEM((SLOTS, HID), BF),
            pltpu.VMEM((NX, SLOTS, FEAT), BF),
            pltpu.VMEM((NX, SLOTS, FEAT), BF),
            *quarter,
            *full,
            *mid,
            *last,
            pltpu.VMEM((NY, 8, 128), F32),
            pltpu.VMEM((3, 8, 128), F32),
            pltpu.VMEM((8, 128), F32),
            pltpu.VMEM((8, 8, 128), F32),
            pltpu.VMEM((NZ, 8, 256), BF),
            pltpu.VMEM((NZ, 8, 256), BF),
            pltpu.SemaphoreType.DMA((148,)),
            pltpu.SemaphoreType.DMA((148,)),
        ],
        compiler_params=pltpu.CompilerParams(
            collective_id=0, has_side_effects=True, vmem_limit_bytes=60 << 20
        ),
    )(*arguments)


def emit_kernel(*refs):
    sources, targets, stage, load_sem, store_sem = refs[:5], refs[5:10], refs[10:15], refs[15], refs[16]
    pieces = [(i, None) for i in range(2)]
    pieces += [(i, part) for part in range(2) for i in range(2, 5)]

    def view(ref, part):
        if part is None:
            return ref
        half = ref.shape[1] // 2
        return ref.at[:, pl.ds(part * half, half)]

    loads = [
        pltpu.make_async_copy(view(sources[i], part), view(stage[i], part), load_sem.at[n])
        for n, (i, part) in enumerate(pieces)
    ]
    stores = [
        pltpu.make_async_copy(view(stage[i], part), view(targets[i], part), store_sem.at[n])
        for n, (i, part) in enumerate(pieces)
    ]
    for copy in loads:
        copy.start()
    for load, store in zip(loads, stores):
        load.wait()
        store.start()
    for copy in stores:
        copy.wait()


def emit(*results):
    return pl.pallas_call(
        emit_kernel,
        name="emit",
        out_shape=tuple(jax.ShapeDtypeStruct(one.shape, one.dtype) for one in results),
        in_specs=[HBM] * 5,
        out_specs=(HBM,) * 5,
        scratch_shapes=[
            *[pltpu.VMEM(one.shape, one.dtype) for one in results],
            pltpu.SemaphoreType.DMA((8,)),
            pltpu.SemaphoreType.DMA((8,)),
        ],
        compiler_params=pltpu.CompilerParams(vmem_limit_bytes=60 << 20),
    )(*results)


def shards(tokens, cotangent, gates, experts, w_gate, w_up, w_down):
    results = layer(tokens, cotangent, gates.T, experts.T, w_gate, w_up, w_down)
    input_grad, routing_grad, gate_grad, up_grad, down_grad = emit(*results)
    return input_grad, routing_grad.T, gate_grad, up_grad, down_grad


def solution(mesh):
    return jax.shard_map(
        shards,
        mesh=mesh,
        in_specs=(
            P("wide", "tensor"),
            P("wide", "tensor"),
            P("wide", None),
            P("wide", None),
            P("wide", None, "tensor"),
            P("wide", None, "tensor"),
            P("wide", "tensor", None),
        ),
        out_specs=(
            P("wide", "tensor"),
            P("wide", None),
            P("wide", None, "tensor"),
            P("wide", None, "tensor"),
            P("wide", "tensor", None),
        ),
        check_vma=False,
    )
```
